512 devices in a mesh: blk: 64 (over y_hi, z, core), event: 8 (over x, y_lo).
Axes of the slice: x: 4, y: 8 (y_hi: 4, y_lo: 2; y = y_hi * 2 + y_lo), z: 8, core: 2. Of those that a mesh axis runs over, the one named last changes fastest.
Arguments:
- adjoint_now: float32 [8, 3, 512, 64, 128], P('event', None, 'blk'), may hold values from -6 to 6
- adjoint_prev: float32 [8, 3, 512, 64, 128], P('event', None, 'blk'), may hold values from -6 to 6
- forward_field: float32 [8, 2, 3, 512, 64, 128], P('event', None, None, 'blk'), may hold values from -6 to 6
- density: float32 [512, 64, 128], P('blk'), may hold values from 0.5 to 2
- lame_first: float32 [512, 64, 128], P('blk'), may hold values from 0.5 to 2
- shear_modulus: float32 [512, 64, 128], P('blk'), may hold values from 0.3 to 1.2
Outputs:
- adjoint_field: float32 [8, 3, 512, 64, 128], P('event', None, 'blk')
- shear_kernel: float32 [512, 64, 128], P('blk', 'event')
- bulk_kernel: float32 [512, 64, 128], P('blk', 'event')
The draws below stay inside these ranges and needn't reach their ends.
All inputs are finite; a program needn't handle non-finite values.
Results may differ from the reference program's by a relative error of at most 0.00002.
Values sent between devices are 32-bit elements; how exact they have to be, the bound alone decides.
A program may use at most 64 MiB of HBM per device.

```python
import math
import jax
import jax.numpy as jnp
from jax import lax

NY = 64
NZ = 128
STEPS = 2
NX = 512
GROUPS = 8


def level_of(rng, shape, split, smallest, high):
    factor_of, own = 1.0, jax.random.fold_in(rng, 6)
    for dim, blocks in split:
        heights = jnp.exp(jax.random.uniform(jax.random.fold_in(own, dim), (blocks,), jnp.float32, smallest / len(split), high / len(split)))
        factor_of = factor_of * jnp.repeat(heights, shape[dim] // blocks).reshape([-1 if axis == dim else 1 for axis in range(len(shape))])
    return factor_of


def centred(key, dims, width, limit, pieces=(), held_as=jnp.bfloat16):
    values = width * jax.random.normal(key, dims, jnp.float32)
    if pieces:
        values = values * level_of(key, dims, pieces, -0.22, 0.18)
    return jnp.clip(values, -limit, limit).astype(held_as)


def setup_inputs(seed: int = 0) -> dict:
    key_of = jax.random.split(jax.random.key(seed), 7)
    adjoint_now = centred(key_of[0], (GROUPS, 3, NX, NY, NZ), 1.0, 6.0, ((0, 8), (2, 64)), jnp.float32)
    adjoint_prev = centred(key_of[1], (GROUPS, 3, NX, NY, NZ), 1.0, 6.0, ((0, 8), (2, 64)), jnp.float32)
    forward_field = centred(key_of[2], (GROUPS, STEPS, 3, NX, NY, NZ), 1.0, 6.0, ((0, 8), (3, 64)), jnp.float32)
    density = jnp.clip(jnp.exp(math.log(2.0) - 1.3862944 * jax.random.uniform(key_of[3], (NX, NY, NZ), jnp.float32) ** level_of(key_of[3], (NX, NY, NZ), ((0, 64),), -0.2, 0.2)), 0.5, 2.0)
    lame_first = jnp.clip(jnp.exp(math.log(2.0) - 1.3862944 * jax.random.uniform(key_of[4], (NX, NY, NZ), jnp.float32) ** level_of(key_of[4], (NX, NY, NZ), ((0, 64),), -0.2, 0.2)), 0.5, 2.0)
    shear_modulus = jnp.clip(jnp.exp(math.log(1.2) - 1.3862944 * jax.random.uniform(key_of[5], (NX, NY, NZ), jnp.float32) ** level_of(key_of[5], (NX, NY, NZ), ((0, 64),), -0.2, 0.2)), 0.3, 1.2)
    return dict(adjoint_now=adjoint_now, adjoint_prev=adjoint_prev, forward_field=forward_field, density=density, lame_first=lame_first, shear_modulus=shear_modulus)


time_step = 0.3


def slope_long(values):
    return (values[2:] - values[:-2]) * 0.5


def slope_mid(values, axis):
    padded = jnp.pad(values, [(1, 1) if dimension == axis else (0, 0) for dimension in range(3)])
    upper = lax.slice_in_dim(padded, 2, padded.shape[axis], axis=axis)
    lower = lax.slice_in_dim(padded, 0, padded.shape[axis] - 2, axis=axis)
    return (upper - lower) * 0.5


def gradient(field):
    table = [[None, None, None], [None, None, None], [None, None, None]]
    for second in range(3):
        component = field[second]
        middle = component[1:-1]
        table[0][second] = slope_long(component)
        table[1][second] = slope_mid(middle, 1)
        table[2][second] = slope_mid(middle, 2)
    return table


def strain_of(table):
    strain = [[0.5 * (table[first][second] + table[second][first]) for second in range(3)] for first in range(3)]
    trace = strain[0][0] + strain[1][1] + strain[2][2]
    return strain, trace


def stress_of(strain, trace, first_lame, shear_part):
    stress = []
    for first in range(3):
        stress_row = []
        for second in range(3):
            entry = 2.0 * shear_part * strain[first][second]
            if first == second:
                entry = entry + first_lame * trace
            stress_row.append(entry)
        stress.append(stress_row)
    return stress


def divergence(stress):
    result = []
    for second in range(3):
        total = slope_long(stress[0][second])
        total = total + slope_mid(stress[1][second], 1)[1:-1]
        total = total + slope_mid(stress[2][second], 2)[1:-1]
        result.append(total)
    return result


def crop(values, count, axis):
    if count == 0:
        return values
    return lax.slice_in_dim(values, count, values.shape[axis] - count, axis=axis)


def kernel_terms(strain, trace, forward_strain, forward_trace, first_lame, shear_part):
    contracted = strain[0][0] * forward_strain[0][0]
    for first in range(3):
        for second in range(3):
            if first + second > 0:
                contracted = contracted + strain[first][second] * forward_strain[first][second]
    shear_term = -2.0 * time_step * shear_part * (contracted - trace * forward_trace / 3.0)
    bulk_term = -time_step * (first_lame + 2.0 * shear_part / 3.0) * trace * forward_trace
    return shear_term, bulk_term


def advance(wide, prev_cut, model_cut, dens_cut, forward_wide, slab_cells):
    strain, trace = strain_of(gradient(wide))
    stress = stress_of(strain, trace, model_cut[0], model_cut[1])
    accel = jnp.stack(divergence(stress))
    updated = 2.0 * crop(wide, 2, 1) - prev_cut + time_step * time_step * accel / dens_cut
    margin = (wide.shape[1] - slab_cells) // 2
    inner = [[crop(entry, margin - 1, 0) for entry in strain_row] for strain_row in strain]
    inner_trace = crop(trace, margin - 1, 0)
    forward_strain, forward_trace = strain_of(gradient(forward_wide))
    model_margin = (model_cut.shape[1] - slab_cells) // 2
    first_lame = crop(model_cut[0], model_margin, 0)
    shear_part = crop(model_cut[1], model_margin, 0)
    return updated, kernel_terms(inner, inner_trace, forward_strain, forward_trace, first_lame, shear_part)


def wrap(values, count, axis):
    size = values.shape[axis]
    head = lax.slice_in_dim(values, size - count, size, axis=axis)
    tail = lax.slice_in_dim(values, 0, count, axis=axis)
    return jnp.concatenate([head, values, tail], axis=axis)


def reference(adjoint_now, adjoint_prev, forward_field, density, lame_first, shear_modulus):
    moduli = jnp.stack([lame_first, shear_modulus])
    model_wide = wrap(moduli, 1, 1)
    shear_total = jnp.zeros(density.shape, jnp.float32)
    bulk_total = jnp.zeros(density.shape, jnp.float32)
    finals = []
    for group in range(GROUPS):
        current = adjoint_now[group]
        former = adjoint_prev[group]
        for step in range(STEPS):
            wide = wrap(current, 2, 1)
            forward_wide = wrap(forward_field[group, step], 1, 1)
            updated, terms = advance(wide, former, model_wide, density, forward_wide, NX)
            shear_total = shear_total + terms[0]
            bulk_total = bulk_total + terms[1]
            former = current
            current = updated
        finals.append(current)
    return jnp.stack(finals), shear_total, bulk_total
```

```python
import functools

import jax
import jax.numpy as jnp
from jax import lax
from jax.experimental import pallas as pl
from jax.experimental.pallas import tpu as pltpu
from jax.sharding import PartitionSpec as P

MESH = pl.DeviceIdType.MESH
time_step = 0.3
PAD = 8
ROWS = 8


def kernel(
    nb, ne, now, prev, fwd, dens, lame, mu, out, sh, bk,
    w0, w1, pv, fw, md, cf, s11, s12, s13, s22, s23, s33, part, got, res,
    lsem, hsend, hrecv, usend, urecv, rsend, rrecv, osem,
):
    layers, height = dens.shape[0], dens.shape[1]
    last = layers - 1
    band = height // ne
    me_b = lax.axis_index("blk")
    me_e = lax.axis_index("event")
    right = lax.rem(me_b + 1, nb)
    left = lax.rem(me_b + nb - 1, nb)
    body = pl.ds(PAD, height)
    chunks = range(0, height, ROWS)

    barrier = pltpu.get_barrier_semaphore()
    for b in (left, right):
        pl.semaphore_signal(barrier, inc=1, device_id={"blk": b}, device_id_type=MESH)
    for k in range(1, ne):
        pl.semaphore_signal(
            barrier, inc=1, device_id={"event": lax.rem(me_e + k, ne)}, device_id_type=MESH
        )

    own = pl.ds(1, layers)
    loc = [
        pltpu.make_async_copy(now.at[0], w0.at[:, pl.ds(2, layers), body], lsem.at[0]),
        pltpu.make_async_copy(mu, md.at[1, own], lsem.at[1]),
        pltpu.make_async_copy(lame, md.at[0, own], lsem.at[2]),
        pltpu.make_async_copy(fwd.at[0, 0], fw.at[0, :, own, body], lsem.at[3]),
        pltpu.make_async_copy(dens, cf, lsem.at[4]),
        pltpu.make_async_copy(prev.at[0], pv, lsem.at[5]),
        pltpu.make_async_copy(fwd.at[0, 1], fw.at[1, :, own, body], lsem.at[6]),
    ]
    for c in loc:
        c.start()

    blank = jnp.zeros((PAD, 128), jnp.float32)
    for top in (0, PAD + height):
        edge = pl.ds(top, PAD)
        for b in range(3):
            for i in range(1, layers + 3):
                w0[b, i, edge, :] = blank
                w1[b, i, edge, :] = blank
            for i in range(1, layers + 1):
                fw[0, b, i, edge, :] = blank
                fw[1, b, i, edge, :] = blank
        for i in range(layers):
            s12[i + 1, edge, :] = blank
            s22[i, edge, :] = blank
            s23[i, edge, :] = blank

    pl.semaphore_wait(barrier, ne + 1)

    def remote(src, dst, ss, rs, dev):
        return pltpu.make_async_remote_copy(
            src_ref=src, dst_ref=dst, send_sem=ss, recv_sem=rs, device_id=dev, device_id_type=MESH
        )

    halo = []
    for side, b in ((0, right), (1, left)):
        dev = {"blk": b}
        e2 = pl.ds(layers - 2, 2) if side == 0 else pl.ds(0, 2)
        e1 = pl.ds(last, 1) if side == 0 else pl.ds(0, 1)
        d2 = pl.ds(0, 2) if side == 0 else pl.ds(layers + 2, 2)
        d1 = pl.ds(0, 1) if side == 0 else pl.ds(layers + 1, 1)
        n = 5 * side
        halo.append([
            remote(now.at[0, :, e2], w0.at[:, d2, body], hsend.at[n], hrecv.at[n], dev),
            remote(mu.at[e1], md.at[1, d1], hsend.at[n + 1], hrecv.at[n + 1], dev),
            remote(lame.at[e1], md.at[0, d1], hsend.at[n + 2], hrecv.at[n + 2], dev),
            remote(fwd.at[0, 0, :, e1], fw.at[0, :, d1, body], hsend.at[n + 3], hrecv.at[n + 3], dev),
            remote(fwd.at[0, 1, :, e1], fw.at[1, :, d1, body], hsend.at[n + 4], hrecv.at[n + 4], dev),
        ])
    for j in range(5):
        halo[0][j].start()
        halo[1][j].start()

    lane = lax.broadcasted_iota(jnp.int32, (ROWS, 128), 1)
    first_lane = lane == 0
    last_lane = lane == 127

    def cross(c):
        return jnp.where(last_lane, 0.0, pltpu.roll(c, 127, 1)) - jnp.where(
            first_lane, 0.0, pltpu.roll(c, 1, 1)
        )

    def grads(u, i, r):
        here, up, down = pl.ds(PAD + r, ROWS), pl.ds(PAD + r + 1, ROWS), pl.ds(PAD + r - 1, ROWS)
        g1 = [u[b, i + 1, here, :] - u[b, i - 1, here, :] for b in range(3)]
        g2 = [u[b, i, up, :] - u[b, i, down, :] for b in range(3)]
        g3 = [cross(u[b, i, here, :]) for b in range(3)]
        return (
            g1[0], g2[1], g3[2], g1[1] + g2[0], g1[2] + g3[0], g2[2] + g3[1],
            g1[0] + g2[1] + g3[2],
        )

    def strain_pass(u, step, i, stress, terms):
        for r in chunks:
            rows = pl.ds(r, ROWS)
            prow = pl.ds(PAD + r, ROWS)
            a, b, c, h12, h13, h23, tr = grads(u, i + 2, r)
            if stress:
                m = md[1, i + 1, rows, :]
                lt = md[0, i + 1, rows, :] * tr
                m2 = m + m
                s11[i + 1, rows, :] = m2 * a + lt
                s12[i + 1, prow, :] = m * h12
                s13[i + 1, rows, :] = m * h13
                if stress == 2:
                    s22[i, prow, :] = m2 * b + lt
                    s23[i, prow, :] = m * h23
                    s33[i, rows, :] = m2 * c + lt
            if terms:
                fa, fb, fc, f12, f13, f23, ft = grads(fw.at[step], i + 1, r)
                bulk = tr * ft
                con = (
                    (a * fa + b * fb + c * fc)
                    + 0.5 * (h12 * f12 + h13 * f13 + h23 * f23)
                    - bulk * (1.0 / 3.0)
                )
                d, q = r // band, pl.ds(r % band, ROWS)
                if step == 0:
                    part[d, 0, i, q, :] = con
                    part[d, 1, i, q, :] = bulk
                else:
                    part[d, 0, i, q, :] += con
                    part[d, 1, i, q, :] += bulk

    def update_pass(u, former, i, store):
        for r in chunks:
            rows = pl.ds(r, ROWS)
            here, up, down = pl.ds(PAD + r, ROWS), pl.ds(PAD + r + 1, ROWS), pl.ds(PAD + r - 1, ROWS)
            k = cf[i, rows, :]
            t1 = (
                (s11[i + 2, rows, :] - s11[i, rows, :])
                + (s12[i + 1, up, :] - s12[i + 1, down, :])
                + cross(s13[i + 1, rows, :])
            )
            t2 = (
                (s12[i + 2, here, :] - s12[i, here, :])
                + (s22[i, up, :] - s22[i, down, :])
                + cross(s23[i, here, :])
            )
            t3 = (
                (s13[i + 2, rows, :] - s13[i, rows, :])
                + (s23[i, up, :] - s23[i, down, :])
                + cross(s33[i, rows, :])
            )
            for b, t in enumerate((t1, t2, t3)):
                store(b, i, r, 2.0 * u[b, i + 2, here, :] - former(b, i, r) + k * t)

    def loop(low, high, f, scale=1, offset=0):
        def step(t, carry):
            f(t * scale + offset)
            return carry

        lax.fori_loop(low, high, step, 0)

    def ends(f, low, high):
        loop(0, 2, f, high - low, low)

    for j in range(4):
        loc[j].wait()
    loop(1, last, lambda i: strain_pass(w0, 0, i, 2, True))
    loc[4].wait()
    loc[5].wait()

    def coefficient(i):
        cf[i] = (0.25 * time_step * time_step) / cf[i]

    loop(0, layers, coefficient)

    def first_former(b, i, r):
        return pv[b, i, pl.ds(r, ROWS), :]

    def first_store(b, i, r, value):
        w1[b, i + 2, pl.ds(PAD + r, ROWS), :] = value

    def first_update(i):
        update_pass(w0, first_former, i, first_store)

    loop(2, layers - 2, first_update)
    for side in (0, 1):
        for j in range(3):
            halo[side][j].wait_recv()
    ends(lambda i: strain_pass(w0, 0, i, 2, False), 0, last)
    ends(lambda i: strain_pass(w0, 0, i, 1, False), -1, layers)
    loop(layers - 2, layers, first_update)
    to_right = remote(
        w1.at[:, pl.ds(layers, 2), body], w1.at[:, pl.ds(0, 2), body],
        usend.at[0], urecv.at[0], {"blk": right},
    )
    to_right.start()
    loop(0, 2, first_update)
    to_left = remote(
        w1.at[:, pl.ds(2, 2), body], w1.at[:, pl.ds(layers + 2, 2), body],
        usend.at[1], urecv.at[1], {"blk": left},
    )
    to_left.start()
    for side in (0, 1):
        halo[side][3].wait_recv()
    ends(lambda i: strain_pass(w0, 0, i, 0, True), 0, last)

    loc[6].wait()
    loop(1, last, lambda i: strain_pass(w1, 1, i, 2, True))
    to_right.wait_recv()
    to_left.wait_recv()
    for side in (0, 1):
        halo[side][4].wait_recv()
    ends(lambda i: strain_pass(w1, 1, i, 2, True), 0, last)
    sums = []
    for k in range(1, ne):
        dest = lax.rem(me_e + k, ne)
        sums.append(remote(part.at[dest], got.at[k], rsend.at[k], rrecv.at[k], {"event": dest}))
        sums[-1].start()
    ends(lambda i: strain_pass(w1, 1, i, 1, False), -1, layers)

    def second_former(b, i, r):
        return w0[b, i + 2, pl.ds(PAD + r, ROWS), :]

    def second_store(b, i, r, value):
        res[b, i, pl.ds(r, ROWS), :] = value

    def out_copy(i):
        return pltpu.make_async_copy(res.at[:, i], out.at[0, :, i], osem.at[i])

    def second_update(i):
        update_pass(w1, second_former, i, second_store)
        out_copy(i).start()

    loop(0, layers, second_update)

    mine = pl.ds(pl.multiple_of(me_e * band, band), band)
    for k in range(ne - 1):
        sums[k].wait_recv()

    def finish(i):
        con = part[me_e, 0, i]
        bulk = part[me_e, 1, i]
        for k in range(1, ne):
            con = con + got[k, 0, i]
            bulk = bulk + got[k, 1, i]
        m = md[1, i + 1, mine, :]
        sh[i] = (-0.5 * time_step) * m * con
        bk[i] = (-0.25 * time_step) * (md[0, i + 1, mine, :] + (2.0 / 3.0) * m) * bulk

    loop(0, layers, finish)

    for i in range(layers):
        out_copy(i).wait()
    for side in (0, 1):
        for c in halo[side]:
            c.wait_send()
    to_right.wait_send()
    to_left.wait_send()
    for c in sums:
        c.wait_send()


def local(nb, ne, adjoint_now, adjoint_prev, forward_field, density, lame_first, shear_modulus):
    layers, height, width = density.shape
    tall = height + 2 * PAD
    band = height // ne
    f32 = jnp.float32
    dma = pltpu.SemaphoreType.DMA
    anywhere = pl.BlockSpec(memory_space=pl.ANY)
    vmem = pl.BlockSpec(memory_space=pltpu.VMEM)
    return pl.pallas_call(
        functools.partial(kernel, nb, ne),
        out_shape=(
            jax.ShapeDtypeStruct((1, 3, layers, height, width), f32),
            jax.ShapeDtypeStruct((layers, band, width), f32),
            jax.ShapeDtypeStruct((layers, band, width), f32),
        ),
        in_specs=[anywhere] * 6,
        out_specs=(anywhere, vmem, vmem),
        scratch_shapes=[
            pltpu.VMEM((3, layers + 4, tall, width), f32),
            pltpu.VMEM((3, layers + 4, tall, width), f32),
            pltpu.VMEM((3, layers, height, width), f32),
            pltpu.VMEM((2, 3, layers + 2, tall, width), f32),
            pltpu.VMEM((2, layers + 2, height, width), f32),
            pltpu.VMEM((layers, height, width), f32),
            pltpu.VMEM((layers + 2, height, width), f32),
            pltpu.VMEM((layers + 2, tall, width), f32),
            pltpu.VMEM((layers + 2, height, width), f32),
            pltpu.VMEM((layers, tall, width), f32),
            pltpu.VMEM((layers, tall, width), f32),
            pltpu.VMEM((layers, height, width), f32),
            pltpu.VMEM((ne, 2, layers, band, width), f32),
            pltpu.VMEM((ne, 2, layers, band, width), f32),
            pltpu.VMEM((3, layers, height, width), f32),
            dma((7,)),
            dma((10,)),
            dma((10,)),
            dma((2,)),
            dma((2,)),
            dma((ne,)),
            dma((ne,)),
            dma((layers,)),
        ],
        compiler_params=pltpu.CompilerParams(collective_id=0, has_side_effects=True),
        name="adjoint",
    )(adjoint_now, adjoint_prev, forward_field, density, lame_first, shear_modulus)


def solution(mesh):
    in_specs = (
        P("event", None, "blk", None, None),
        P("event", None, "blk", None, None),
        P("event", None, None, "blk", None, None),
        P("blk", None, None),
        P("blk", None, None),
        P("blk", None, None),
    )
    out_specs = (
        P("event", None, "blk", None, None),
        P("blk", "event", None),
        P("blk", "event", None),
    )
    body = functools.partial(local, mesh.shape["blk"], mesh.shape["event"])
    return jax.shard_map(body, mesh=mesh, in_specs=in_specs, out_specs=out_specs, check_vma=False)
```

```python
import functools

import jax
import jax.numpy as jnp
from jax import lax
from jax.experimental import pallas as pl
from jax.experimental.pallas import tpu as pltpu
from jax.sharding import PartitionSpec as P

MESH = pl.DeviceIdType.MESH
time_step = 0.3
PAD = 8
ROWS = 8


def kernel(
    nb, ne, now, prev, fwd, dens, lame, mu, res, sh, bk,
    w0, w1, pv, fw, md, cf, s11, s12, s13, s22, s23, s33, part, got,
    lsem, hsend, hrecv, usend, urecv, rsend, rrecv,
):
    layers, height = dens.shape[0], dens.shape[1]
    last = layers - 1
    band = height // ne
    me_b = lax.axis_index("blk")
    me_e = lax.axis_index("event")
    right = lax.rem(me_b + 1, nb)
    left = lax.rem(me_b + nb - 1, nb)
    body = pl.ds(PAD, height)
    chunks = range(0, height, ROWS)

    barrier = pltpu.get_barrier_semaphore()
    for b in (left, right):
        pl.semaphore_signal(barrier, inc=1, device_id={"blk": b}, device_id_type=MESH)
    for k in range(1, ne):
        pl.semaphore_signal(
            barrier, inc=1, device_id={"event": lax.rem(me_e + k, ne)}, device_id_type=MESH
        )

    own = pl.ds(1, layers)
    loc = [
        pltpu.make_async_copy(now.at[0], w0.at[:, pl.ds(2, layers), body], lsem.at[0]),
        pltpu.make_async_copy(mu, md.at[1, own], lsem.at[1]),
        pltpu.make_async_copy(lame, md.at[0, own], lsem.at[2]),
        pltpu.make_async_copy(fwd.at[0, 0], fw.at[0, :, own, body], lsem.at[3]),
        pltpu.make_async_copy(dens, cf, lsem.at[4]),
        pltpu.make_async_copy(prev.at[0], pv, lsem.at[5]),
        pltpu.make_async_copy(fwd.at[0, 1], fw.at[1, :, own, body], lsem.at[6]),
    ]
    for j in range(3):
        loc[j].start()

    pl.semaphore_wait(barrier, ne + 1)

    def remote(src, dst, ss, rs, dev):
        return pltpu.make_async_remote_copy(
            src_ref=src, dst_ref=dst, send_sem=ss, recv_sem=rs, device_id=dev, device_id_type=MESH
        )

    halo = []
    for side, b in ((0, right), (1, left)):
        dev = {"blk": b}
        e2 = pl.ds(layers - 2, 2) if side == 0 else pl.ds(0, 2)
        e1 = pl.ds(last, 1) if side == 0 else pl.ds(0, 1)
        d2 = pl.ds(0, 2) if side == 0 else pl.ds(layers + 2, 2)
        d1 = pl.ds(0, 1) if side == 0 else pl.ds(layers + 1, 1)
        n = 5 * side
        halo.append([
            remote(now.at[0, :, e2], w0.at[:, d2, body], hsend.at[n], hrecv.at[n], dev),
            remote(mu.at[e1], md.at[1, d1], hsend.at[n + 1], hrecv.at[n + 1], dev),
            remote(lame.at[e1], md.at[0, d1], hsend.at[n + 2], hrecv.at[n + 2], dev),
            remote(fwd.at[0, 0, :, e1], fw.at[0, :, d1, body], hsend.at[n + 3], hrecv.at[n + 3], dev),
            remote(fwd.at[0, 1, :, e1], fw.at[1, :, d1, body], hsend.at[n + 4], hrecv.at[n + 4], dev),
        ])
    for j in range(5):
        halo[0][j].start()
        halo[1][j].start()

    for j in range(3, 7):
        loc[j].start()

    blank = jnp.zeros((PAD, 128), jnp.float32)
    for top in (0, PAD + height):
        edge = pl.ds(top, PAD)
        for b in range(3):
            for i in range(1, layers + 3):
                w0[b, i, edge, :] = blank
                w1[b, i, edge, :] = blank
            for i in range(1, layers + 1):
                fw[0, b, i, edge, :] = blank
                fw[1, b, i, edge, :] = blank
        for i in range(layers):
            s12[i + 1, edge, :] = blank
            s22[i, edge, :] = blank
            s23[i, edge, :] = blank

    lane = lax.broadcasted_iota(jnp.int32, (ROWS, 128), 1)
    first_lane = lane == 0
    last_lane = lane == 127

    def cross(c):
        return jnp.where(last_lane, 0.0, pltpu.roll(c, 127, 1)) - jnp.where(
            first_lane, 0.0, pltpu.roll(c, 1, 1)
        )

    def grads(u, i, r):
        here, up, down = pl.ds(PAD + r, ROWS), pl.ds(PAD + r + 1, ROWS), pl.ds(PAD + r - 1, ROWS)
        g1 = [u[b, i + 1, here, :] - u[b, i - 1, here, :] for b in range(3)]
        g2 = [u[b, i, up, :] - u[b, i, down, :] for b in range(3)]
        g3 = [cross(u[b, i, here, :]) for b in range(3)]
        return (
            g1[0], g2[1], g3[2], g1[1] + g2[0], g1[2] + g3[0], g2[2] + g3[1],
            g1[0] + g2[1] + g3[2],
        )

    def strain_pass(u, step, i, stress, place=None):
        for r in chunks:
            rows = pl.ds(r, ROWS)
            prow = pl.ds(PAD + r, ROWS)
            a, b, c, h12, h13, h23, tr = grads(u, i + 2, r)
            if stress:
                m = md[1, i + 1, rows, :]
                lt = md[0, i + 1, rows, :] * tr
                m2 = m + m
                s11[i + 1, rows, :] = m2 * a + lt
                s12[i + 1, prow, :] = m * h12
                s13[i + 1, rows, :] = m * h13
                if stress == 2:
                    s22[i, prow, :] = m2 * b + lt
                    s23[i, prow, :] = m * h23
                    s33[i, rows, :] = m2 * c + lt
            if place is not None:
                fa, fb, fc, f12, f13, f23, ft = grads(fw.at[step], i + 1, r)
                bulk = tr * ft
                con = (
                    (a * fa + b * fb + c * fc)
                    + 0.5 * (h12 * f12 + h13 * f13 + h23 * f23)
                    - bulk * (1.0 / 3.0)
                )
                d, q = r // band, pl.ds(r % band, ROWS)
                if step == 0:
                    part[d, place, 0, q, :] = con
                    part[d, place, 1, q, :] = bulk
                else:
                    part[d, place, 0, q, :] += con
                    part[d, place, 1, q, :] += bulk

    def update_pass(u, former, i, store):
        for r in chunks:
            rows = pl.ds(r, ROWS)
            here, up, down = pl.ds(PAD + r, ROWS), pl.ds(PAD + r + 1, ROWS), pl.ds(PAD + r - 1, ROWS)
            k = cf[i, rows, :]
            t1 = (
                (s11[i + 2, rows, :] - s11[i, rows, :])
                + (s12[i + 1, up, :] - s12[i + 1, down, :])
                + cross(s13[i + 1, rows, :])
            )
            t2 = (
                (s12[i + 2, here, :] - s12[i, here, :])
                + (s22[i, up, :] - s22[i, down, :])
                + cross(s23[i, here, :])
            )
            t3 = (
                (s13[i + 2, rows, :] - s13[i, rows, :])
                + (s23[i, up, :] - s23[i, down, :])
                + cross(s33[i, rows, :])
            )
            for b, t in enumerate((t1, t2, t3)):
                store(b, i, r, 2.0 * u[b, i + 2, here, :] - former(b, i, r) + k * t)

    def loop(low, high, f):
        def step(t, carry):
            f(t)
            return carry

        lax.fori_loop(low, high, step, 0)

    def first_former(b, i, r):
        return pv[b, i, pl.ds(r, ROWS), :]

    def first_store(b, i, r, value):
        w1[b, i + 2, pl.ds(PAD + r, ROWS), :] = value

    def first_update(i):
        update_pass(w0, first_former, i, first_store)

    def second_former(b, i, r):
        return w0[b, i + 2, pl.ds(PAD + r, ROWS), :]

    def second_store(b, i, r, value):
        res[b, i, pl.ds(r, ROWS), :] = value

    def second_update(i):
        update_pass(w1, second_former, i, second_store)

    sums = []

    def send_terms(group, low, count):
        for k in range(1, ne):
            dest = lax.rem(me_e + k, ne)
            n = group * ne + k
            sums.append(remote(
                part.at[dest, pl.ds(low, count)], got.at[k, pl.ds(low, count)],
                rsend.at[n], rrecv.at[n], {"event": dest},
            ))
            sums[-1].start()

    for j in range(4):
        loc[j].wait()
    loop(1, 3, lambda i: strain_pass(w0, 0, i, 2, i + 1))
    loop(3, 5, lambda i: strain_pass(w0, 0, i, 2, i - 3))
    loop(5, 7, lambda i: strain_pass(w0, 0, i, 2, i - 1))
    loc[4].wait()
    loc[5].wait()

    def coefficient(i):
        cf[i] = (0.25 * time_step * time_step) / cf[i]

    loop(0, layers, coefficient)
    loop(2, 6, first_update)
    loc[6].wait()
    loop(3, 5, lambda i: strain_pass(w1, 1, i, 2, i - 3))
    send_terms(0, 0, 2)

    for side in (0, 1):
        for j in range(3):
            halo[side][j].wait_recv()
    loop(0, 2, lambda t: strain_pass(w0, 0, last * t, 2))
    loop(0, 2, lambda t: strain_pass(w0, 0, (layers + 1) * t - 1, 1))
    loop(6, 8, first_update)
    to_right = remote(
        w1.at[:, pl.ds(layers, 2), body], w1.at[:, pl.ds(0, 2), body],
        usend.at[0], urecv.at[0], {"blk": right},
    )
    to_right.start()
    loop(0, 2, first_update)
    to_left = remote(
        w1.at[:, pl.ds(2, 2), body], w1.at[:, pl.ds(layers + 2, 2), body],
        usend.at[1], urecv.at[1], {"blk": left},
    )
    to_left.start()

    loop(1, 3, lambda i: strain_pass(w1, 1, i, 2, i + 1))
    loop(5, 7, lambda i: strain_pass(w1, 1, i, 2, i - 1))
    send_terms(1, 2, 4)
    for side in (0, 1):
        halo[side][3].wait_recv()
    loop(0, 2, lambda t: strain_pass(w0, 0, last * t, 0, 6 + t))
    loop(2, 6, second_update)

    to_right.wait_recv()
    to_left.wait_recv()
    for side in (0, 1):
        halo[side][4].wait_recv()
    loop(0, 2, lambda t: strain_pass(w1, 1, last * t, 2, 6 + t))
    send_terms(2, 6, 2)
    loop(0, 2, lambda t: strain_pass(w1, 1, (layers + 1) * t - 1, 1))
    loop(0, 2, second_update)
    loop(6, 8, second_update)

    mine = pl.ds(pl.multiple_of(me_e * band, band), band)
    for c in sums:
        c.wait_recv()
    for p, i in enumerate((3, 4, 1, 2, 5, 6, 0, 7)):
        con = part[me_e, p, 0]
        bulk = part[me_e, p, 1]
        for k in range(1, ne):
            con = con + got[k, p, 0]
            bulk = bulk + got[k, p, 1]
        m = md[1, i + 1, mine, :]
        sh[i] = (-0.5 * time_step) * m * con
        bk[i] = (-0.25 * time_step) * (md[0, i + 1, mine, :] + (2.0 / 3.0) * m) * bulk

    for side in (0, 1):
        for c in halo[side]:
            c.wait_send()
    to_right.wait_send()
    to_left.wait_send()
    for c in sums:
        c.wait_send()


def put_out(field, shear, bulk, field_out, shear_out, bulk_out, sem):
    copies = [
        pltpu.make_async_copy(field, field_out.at[0], sem.at[0]),
        pltpu.make_async_copy(shear, shear_out, sem.at[1]),
        pltpu.make_async_copy(bulk, bulk_out, sem.at[2]),
    ]
    for c in copies:
        c.start()
    for c in copies:
        c.wait()


def local(nb, ne, adjoint_now, adjoint_prev, forward_field, density, lame_first, shear_modulus):
    layers, height, width = density.shape
    tall = height + 2 * PAD
    band = height // ne
    f32 = jnp.float32
    dma = pltpu.SemaphoreType.DMA
    anywhere = pl.BlockSpec(memory_space=pl.ANY)
    vmem = pl.BlockSpec(memory_space=pltpu.VMEM)
    results = pl.pallas_call(
        functools.partial(kernel, nb, ne),
        out_shape=(
            pltpu.VMEM((3, layers, height, width), f32),
            pltpu.VMEM((layers, band, width), f32),
            pltpu.VMEM((layers, band, width), f32),
        ),
        in_specs=[anywhere] * 6,
        out_specs=(vmem,) * 3,
        scratch_shapes=[
            pltpu.VMEM((3, layers + 4, tall, width), f32),
            pltpu.VMEM((3, layers + 4, tall, width), f32),
            pltpu.VMEM((3, layers, height, width), f32),
            pltpu.VMEM((2, 3, layers + 2, tall, width), f32),
            pltpu.VMEM((2, layers + 2, height, width), f32),
            pltpu.VMEM((layers, height, width), f32),
            pltpu.VMEM((layers + 2, height, width), f32),
            pltpu.VMEM((layers + 2, tall, width), f32),
            pltpu.VMEM((layers + 2, height, width), f32),
            pltpu.VMEM((layers, tall, width), f32),
            pltpu.VMEM((layers, tall, width), f32),
            pltpu.VMEM((layers, height, width), f32),
            pltpu.VMEM((ne, layers, 2, band, width), f32),
            pltpu.VMEM((ne, layers, 2, band, width), f32),
            dma((7,)),
            dma((10,)),
            dma((10,)),
            dma((2,)),
            dma((2,)),
            dma((3 * ne,)),
            dma((3 * ne,)),
        ],
        compiler_params=pltpu.CompilerParams(collective_id=0, has_side_effects=True),
        name="adjoint",
    )(adjoint_now, adjoint_prev, forward_field, density, lame_first, shear_modulus)
    return pl.pallas_call(
        put_out,
        out_shape=(
            jax.ShapeDtypeStruct((1, 3, layers, height, width), f32),
            jax.ShapeDtypeStruct((layers, band, width), f32),
            jax.ShapeDtypeStruct((layers, band, width), f32),
        ),
        in_specs=[anywhere] * 3,
        out_specs=(anywhere,) * 3,
        scratch_shapes=[dma((3,))],
        compiler_params=pltpu.CompilerParams(vmem_limit_bytes=1 << 20),
        name="put_out",
    )(*results)


def solution(mesh):
    in_specs = (
        P("event", None, "blk", None, None),
        P("event", None, "blk", None, None),
        P("event", None, None, "blk", None, None),
        P("blk", None, None),
        P("blk", None, None),
        P("blk", None, None),
    )
    out_specs = (
        P("event", None, "blk", None, None),
        P("blk", "event", None),
        P("blk", "event", None),
    )
    body = functools.partial(local, mesh.shape["blk"], mesh.shape["event"])
    return jax.shard_map(body, mesh=mesh, in_specs=in_specs, out_specs=out_specs, check_vma=False)
```

```python
import functools

import jax
import jax.numpy as jnp
from jax import lax
from jax.experimental import pallas as pl
from jax.experimental.pallas import tpu as pltpu
from jax.sharding import PartitionSpec as P

MESH = pl.DeviceIdType.MESH
time_step = 0.3
PAD = 8
ROWS = 8


def kernel(
    nb, ne, run, now, prev, fwd, dens, lame, mu, res, sh, bk,
    w0, w1, pv, fw, md, cf, s11, s12, s13, s22, s23, s33, part, got, passed,
    lsem, hsend, hrecv, usend, urecv, rsend, rrecv, psend, precv, fsend,
):
    layers, height = dens.shape[0], dens.shape[1]
    last = layers - 1
    band = height // ne
    me_b = lax.axis_index("blk")
    me_e = lax.axis_index("event")
    right = lax.rem(me_b + 1, nb)
    left = lax.rem(me_b + nb - 1, nb)
    body = pl.ds(PAD, height)

    spot = lax.rem(me_b, run)
    is_head = spot == 0
    is_tail = spot == run - 1
    at_edge = jnp.logical_or(is_head, is_tail)
    tail = lax.div(spot, run - 1)
    mirror = me_b - spot + (run - 1 - spot)
    beyond = lax.rem(me_b + run * (1 - 2 * tail) + nb, nb)
    chunks = range(0, height, ROWS)

    barrier = pltpu.get_barrier_semaphore()
    for b in (left, right, mirror, lax.rem(me_b + run, nb), lax.rem(me_b + nb - run, nb)):
        pl.semaphore_signal(barrier, inc=1, device_id={"blk": b}, device_id_type=MESH)
    for k in range(1, ne):
        pl.semaphore_signal(
            barrier, inc=1, device_id={"event": lax.rem(me_e + k, ne)}, device_id_type=MESH
        )

    own = pl.ds(1, layers)
    loc = [
        pltpu.make_async_copy(now.at[0], w0.at[:, pl.ds(2, layers), body], lsem.at[0]),
        pltpu.make_async_copy(mu, md.at[1, own], lsem.at[1]),
        pltpu.make_async_copy(lame, md.at[0, own], lsem.at[2]),
        pltpu.make_async_copy(fwd.at[0, 0], fw.at[0, :, own, body], lsem.at[3]),
        pltpu.make_async_copy(dens, cf, lsem.at[4]),
        pltpu.make_async_copy(prev.at[0], pv, lsem.at[5]),
        pltpu.make_async_copy(fwd.at[0, 1], fw.at[1, :, own, body], lsem.at[6]),
    ]
    for j in range(3):
        loc[j].start()

    pl.semaphore_wait(barrier, ne + 4)

    def remote(src, dst, ss, rs, dev):
        return pltpu.make_async_remote_copy(
            src_ref=src, dst_ref=dst, send_sem=ss, recv_sem=rs, device_id=dev, device_id_type=MESH
        )

    halo = []
    for side, b in ((0, right), (1, left)):
        dev = {"blk": b}
        e2 = pl.ds(layers - 2, 2) if side == 0 else pl.ds(0, 2)
        e1 = pl.ds(last, 1) if side == 0 else pl.ds(0, 1)
        d2 = pl.ds(0, 2) if side == 0 else pl.ds(layers + 2, 2)
        d1 = pl.ds(0, 1) if side == 0 else pl.ds(layers + 1, 1)
        n = 5 * side
        halo.append([
            remote(now.at[0, :, e2], w0.at[:, d2, body], hsend.at[n], hrecv.at[n], dev),
            remote(mu.at[e1], md.at[1, d1], hsend.at[n + 1], hrecv.at[n + 1], dev),
            remote(lame.at[e1], md.at[0, d1], hsend.at[n + 2], hrecv.at[n + 2], dev),
            remote(fwd.at[0, 0, :, e1], fw.at[0, :, d1, body], hsend.at[n + 3], hrecv.at[n + 3], dev),
            remote(fwd.at[0, 1, :, e1], fw.at[1, :, d1, body], hsend.at[n + 4], hrecv.at[n + 4], dev),
        ])
    for j in range(3):
        halo[0][j].start()
        halo[1][j].start()
    edge_layer = pl.ds(last * tail, 1)
    handed = [
        remote(fwd.at[0, j, :, edge_layer], passed.at[j], psend.at[j], precv.at[j], {"blk": mirror})
        for j in range(2)
    ]
    far_layer = pl.ds((layers + 1) * tail, 1)
    onward = [
        remote(
            passed.at[j], fw.at[j, :, far_layer, body], fsend.at[j], hrecv.at[5 * tail + 3 + j],
            {"blk": beyond},
        )
        for j in range(2)
    ]

    @pl.when(at_edge)
    def _():
        for c in handed:
            c.start()

    @pl.when(jnp.logical_not(is_tail))
    def _():
        halo[0][3].start()
        halo[0][4].start()

    @pl.when(jnp.logical_not(is_head))
    def _():
        halo[1][3].start()
        halo[1][4].start()

    for j in range(3, 7):
        loc[j].start()

    blank = jnp.zeros((PAD, 128), jnp.float32)
    for top in (0, PAD + height):
        edge = pl.ds(top, PAD)
        for b in range(3):
            for i in range(1, layers + 3):
                w0[b, i, edge, :] = blank
                w1[b, i, edge, :] = blank
            for i in range(1, layers + 1):
                fw[0, b, i, edge, :] = blank
                fw[1, b, i, edge, :] = blank
        for i in range(layers):
            s12[i + 1, edge, :] = blank
            s22[i, edge, :] = blank
            s23[i, edge, :] = blank

    lane = lax.broadcasted_iota(jnp.int32, (ROWS, 128), 1)
    first_lane = lane == 0
    last_lane = lane == 127

    def cross(c):
        return jnp.where(last_lane, 0.0, pltpu.roll(c, 127, 1)) - jnp.where(
            first_lane, 0.0, pltpu.roll(c, 1, 1)
        )

    def grads(u, i, r):
        here, up, down = pl.ds(PAD + r, ROWS), pl.ds(PAD + r + 1, ROWS), pl.ds(PAD + r - 1, ROWS)
        g1 = [u[b, i + 1, here, :] - u[b, i - 1, here, :] for b in range(3)]
        g2 = [u[b, i, up, :] - u[b, i, down, :] for b in range(3)]
        g3 = [cross(u[b, i, here, :]) for b in range(3)]
        return (
            g1[0], g2[1], g3[2], g1[1] + g2[0], g1[2] + g3[0], g2[2] + g3[1],
            g1[0] + g2[1] + g3[2],
        )

    def strain_pass(u, step, i, stress, place=None):
        for r in chunks:
            rows = pl.ds(r, ROWS)
            prow = pl.ds(PAD + r, ROWS)
            a, b, c, h12, h13, h23, tr = grads(u, i + 2, r)
            if stress:
                m = md[1, i + 1, rows, :]
                lt = md[0, i + 1, rows, :] * tr
                m2 = m + m
                s11[i + 1, rows, :] = m2 * a + lt
                s12[i + 1, prow, :] = m * h12
                s13[i + 1, rows, :] = m * h13
                if stress == 2:
                    s22[i, prow, :] = m2 * b + lt
                    s23[i, prow, :] = m * h23
                    s33[i, rows, :] = m2 * c + lt
            if place is not None:
                fa, fb, fc, f12, f13, f23, ft = grads(fw.at[step], i + 1, r)
                bulk = tr * ft
                con = (
                    (a * fa + b * fb + c * fc)
                    + 0.5 * (h12 * f12 + h13 * f13 + h23 * f23)
                    - bulk * (1.0 / 3.0)
                )
                d, q = r // band, pl.ds(r % band, ROWS)
                if step == 0:
                    part[d, place, 0, q, :] = con
                    part[d, place, 1, q, :] = bulk
                else:
                    part[d, place, 0, q, :] += con
                    part[d, place, 1, q, :] += bulk

    def update_pass(u, former, i, store):
        for r in chunks:
            rows = pl.ds(r, ROWS)
            here, up, down = pl.ds(PAD + r, ROWS), pl.ds(PAD + r + 1, ROWS), pl.ds(PAD + r - 1, ROWS)
            k = cf[i, rows, :]
            t1 = (
                (s11[i + 2, rows, :] - s11[i, rows, :])
                + (s12[i + 1, up, :] - s12[i + 1, down, :])
                + cross(s13[i + 1, rows, :])
            )
            t2 = (
                (s12[i + 2, here, :] - s12[i, here, :])
                + (s22[i, up, :] - s22[i, down, :])
                + cross(s23[i, here, :])
            )
            t3 = (
                (s13[i + 2, rows, :] - s13[i, rows, :])
                + (s23[i, up, :] - s23[i, down, :])
                + cross(s33[i, rows, :])
            )
            for b, t in enumerate((t1, t2, t3)):
                store(b, i, r, 2.0 * u[b, i + 2, here, :] - former(b, i, r) + k * t)

    def loop(low, high, f):
        def step(t, carry):
            f(t)
            return carry

        lax.fori_loop(low, high, step, 0)

    def first_former(b, i, r):
        return pv[b, i, pl.ds(r, ROWS), :]

    def first_store(b, i, r, value):
        w1[b, i + 2, pl.ds(PAD + r, ROWS), :] = value

    def first_update(i):
        update_pass(w0, first_former, i, first_store)

    def second_former(b, i, r):
        return w0[b, i + 2, pl.ds(PAD + r, ROWS), :]

    def second_store(b, i, r, value):
        res[b, i, pl.ds(r, ROWS), :] = value

    def second_update(i):
        update_pass(w1, second_former, i, second_store)

    sums = []

    def send_terms(group, low, count):
        for k in range(1, ne):
            dest = lax.rem(me_e + k, ne)
            n = group * ne + k
            sums.append(remote(
                part.at[dest, pl.ds(low, count)], got.at[k, pl.ds(low, count)],
                rsend.at[n], rrecv.at[n], {"event": dest},
            ))
            sums[-1].start()

    for j in range(4):
        loc[j].wait()
    loop(1, 3, lambda i: strain_pass(w0, 0, i, 2, i + 1))
    loop(3, 5, lambda i: strain_pass(w0, 0, i, 2, i - 3))
    loop(5, 7, lambda i: strain_pass(w0, 0, i, 2, i - 1))
    loc[4].wait()
    loc[5].wait()

    def coefficient(i):
        cf[i] = (0.25 * time_step * time_step) / cf[i]

    loop(0, layers, coefficient)
    loop(2, 6, first_update)

    @pl.when(at_edge)
    def _():
        for j in range(2):
            handed[j].wait_recv()
            onward[j].start()

    loc[6].wait()
    loop(3, 5, lambda i: strain_pass(w1, 1, i, 2, i - 3))
    send_terms(0, 0, 2)

    for side in (0, 1):
        for j in range(3):
            halo[side][j].wait_recv()
    loop(0, 2, lambda t: strain_pass(w0, 0, last * t, 2))
    loop(0, 2, lambda t: strain_pass(w0, 0, (layers + 1) * t - 1, 1))
    loop(6, 8, first_update)
    def edge_copy(source, target, n, b):
        return remote(
            w1.at[:, pl.ds(source, 1), body], w1.at[:, pl.ds(target, 1), body],
            usend.at[n], urecv.at[n], {"blk": b},
        )

    near = [edge_copy(layers + 1, 1, 0, right), edge_copy(2, layers + 2, 1, left)]
    far = [edge_copy(layers, 0, 2, right), edge_copy(3, layers + 3, 3, left)]
    near[0].start()
    far[0].start()
    loop(0, 2, first_update)
    near[1].start()
    far[1].start()

    loop(1, 3, lambda i: strain_pass(w1, 1, i, 2, i + 1))
    loop(5, 7, lambda i: strain_pass(w1, 1, i, 2, i - 1))
    send_terms(1, 2, 4)
    for side in (0, 1):
        halo[side][3].wait_recv()
    loop(0, 2, lambda t: strain_pass(w0, 0, last * t, 0, 6 + t))
    loop(2, 6, second_update)

    for c in near:
        c.wait_recv()
    for side in (0, 1):
        halo[side][4].wait_recv()
    loop(0, 2, lambda t: strain_pass(w1, 1, last * t, 2, 6 + t))
    send_terms(2, 6, 2)
    for c in far:
        c.wait_recv()
    loop(0, 2, lambda t: strain_pass(w1, 1, (layers + 1) * t - 1, 1))
    loop(0, 2, second_update)
    loop(6, 8, second_update)

    mine = pl.ds(pl.multiple_of(me_e * band, band), band)
    for c in sums:
        c.wait_recv()
    for p, i in enumerate((3, 4, 1, 2, 5, 6, 0, 7)):
        con = part[me_e, p, 0]
        bulk = part[me_e, p, 1]
        for k in range(1, ne):
            con = con + got[k, p, 0]
            bulk = bulk + got[k, p, 1]
        m = md[1, i + 1, mine, :]
        sh[i] = (-0.5 * time_step) * m * con
        bk[i] = (-0.25 * time_step) * (md[0, i + 1, mine, :] + (2.0 / 3.0) * m) * bulk

    for side in (0, 1):
        for c in halo[side][:3]:
            c.wait_send()

    @pl.when(at_edge)
    def _():
        for c in handed + onward:
            c.wait_send()

    @pl.when(jnp.logical_not(is_tail))
    def _():
        halo[0][3].wait_send()
        halo[0][4].wait_send()

    @pl.when(jnp.logical_not(is_head))
    def _():
        halo[1][3].wait_send()
        halo[1][4].wait_send()

    for c in near + far:
        c.wait_send()
    for c in sums:
        c.wait_send()


def put_out(field, shear, bulk, field_out, shear_out, bulk_out, sem):
    copies = [
        pltpu.make_async_copy(field, field_out.at[0], sem.at[0]),
        pltpu.make_async_copy(shear, shear_out, sem.at[1]),
        pltpu.make_async_copy(bulk, bulk_out, sem.at[2]),
    ]
    for c in copies:
        c.start()
    for c in copies:
        c.wait()


def local(nb, ne, adjoint_now, adjoint_prev, forward_field, density, lame_first, shear_modulus):
    layers, height, width = density.shape
    tall = height + 2 * PAD
    band = height // ne
    run = 16 if nb % 16 == 0 else 2
    f32 = jnp.float32
    dma = pltpu.SemaphoreType.DMA
    anywhere = pl.BlockSpec(memory_space=pl.ANY)
    vmem = pl.BlockSpec(memory_space=pltpu.VMEM)
    results = pl.pallas_call(
        functools.partial(kernel, nb, ne, run),
        out_shape=(
            pltpu.VMEM((3, layers, height, width), f32),
            pltpu.VMEM((layers, band, width), f32),
            pltpu.VMEM((layers, band, width), f32),
        ),
        in_specs=[anywhere] * 6,
        out_specs=(vmem,) * 3,
        scratch_shapes=[
            pltpu.VMEM((3, layers + 4, tall, width), f32),
            pltpu.VMEM((3, layers + 4, tall, width), f32),
            pltpu.VMEM((3, layers, height, width), f32),
            pltpu.VMEM((2, 3, layers + 2, tall, width), f32),
            pltpu.VMEM((2, layers + 2, height, width), f32),
            pltpu.VMEM((layers, height, width), f32),
            pltpu.VMEM((layers + 2, height, width), f32),
            pltpu.VMEM((layers + 2, tall, width), f32),
            pltpu.VMEM((layers + 2, height, width), f32),
            pltpu.VMEM((layers, tall, width), f32),
            pltpu.VMEM((layers, tall, width), f32),
            pltpu.VMEM((layers, height, width), f32),
            pltpu.VMEM((ne, layers, 2, band, width), f32),
            pltpu.VMEM((ne, layers, 2, band, width), f32),
            pltpu.VMEM((2, 3, 1, height, width), f32),
            dma((7,)),
            dma((10,)),
            dma((10,)),
            dma((4,)),
            dma((4,)),
            dma((3 * ne,)),
            dma((3 * ne,)),
            dma((2,)),
            dma((2,)),
            dma((2,)),
        ],
        compiler_params=pltpu.CompilerParams(collective_id=0, has_side_effects=True),
        name="adjoint",
    )(adjoint_now, adjoint_prev, forward_field, density, lame_first, shear_modulus)
    return pl.pallas_call(
        put_out,
        out_shape=(
            jax.ShapeDtypeStruct((1, 3, layers, height, width), f32),
            jax.ShapeDtypeStruct((layers, band, width), f32),
            jax.ShapeDtypeStruct((layers, band, width), f32),
        ),
        in_specs=[anywhere] * 3,
        out_specs=(anywhere,) * 3,
        scratch_shapes=[dma((3,))],
        compiler_params=pltpu.CompilerParams(vmem_limit_bytes=1 << 20),
        name="put_out",
    )(*results)


def solution(mesh):
    in_specs = (
        P("event", None, "blk", None, None),
        P("event", None, "blk", None, None),
        P("event", None, None, "blk", None, None),
        P("blk", None, None),
        P("blk", None, None),
        P("blk", None, None),
    )
    out_specs = (
        P("event", None, "blk", None, None),
        P("blk", "event", None),
        P("blk", "event", None),
    )
    body = functools.partial(local, mesh.shape["blk"], mesh.shape["event"])
    return jax.shard_map(body, mesh=mesh, in_specs=in_specs, out_specs=out_specs, check_vma=False)
```

```python
import functools

import jax
import jax.numpy as jnp
from jax import lax
from jax.experimental import pallas as pl
from jax.experimental.pallas import tpu as pltpu
from jax.sharding import PartitionSpec as P

MESH = pl.DeviceIdType.MESH
time_step = 0.3
PAD = 8
ROWS = 8


def kernel(
    nb, ne, run, now, prev, fwd, dens, lame, mu, res, sh, bk,
    w0, w1, pv, fw, md, cf, s11, s12, s13, s22, s23, s33, part, got, passed, passed_now,
    lsem, hsend, hrecv, usend, urecv, rsend, rrecv, psend, precv, fsend,
):
    layers, height = dens.shape[0], dens.shape[1]
    last = layers - 1
    band = height // ne
    me_b = lax.axis_index("blk")
    me_e = lax.axis_index("event")
    right = lax.rem(me_b + 1, nb)
    left = lax.rem(me_b + nb - 1, nb)
    body = pl.ds(PAD, height)

    spot = lax.rem(me_b, run)
    is_head = spot == 0
    is_tail = spot == run - 1
    at_edge = jnp.logical_or(is_head, is_tail)
    tail = lax.div(spot, run - 1)
    mirror = me_b - spot + (run - 1 - spot)
    beyond = lax.rem(me_b + run * (1 - 2 * tail) + nb, nb)
    chunks = range(0, height, ROWS)

    barrier = pltpu.get_barrier_semaphore()
    for b in (left, right, mirror, lax.rem(me_b + run, nb), lax.rem(me_b + nb - run, nb)):
        pl.semaphore_signal(barrier, inc=1, device_id={"blk": b}, device_id_type=MESH)
    for k in range(1, ne):
        pl.semaphore_signal(
            barrier, inc=1, device_id={"event": lax.rem(me_e + k, ne)}, device_id_type=MESH
        )

    own = pl.ds(1, layers)
    loc = [
        pltpu.make_async_copy(now.at[0], w0.at[:, pl.ds(2, layers), body], lsem.at[0]),
        pltpu.make_async_copy(mu, md.at[1, own], lsem.at[1]),
        pltpu.make_async_copy(lame, md.at[0, own], lsem.at[2]),
        pltpu.make_async_copy(fwd.at[0, 0], fw.at[0, :, own, body], lsem.at[3]),
        pltpu.make_async_copy(dens, cf, lsem.at[4]),
        pltpu.make_async_copy(prev.at[0], pv, lsem.at[5]),
        pltpu.make_async_copy(fwd.at[0, 1], fw.at[1, :, own, body], lsem.at[6]),
    ]
    for j in range(3):
        loc[j].start()

    pl.semaphore_wait(barrier, ne + 4)

    def remote(src, dst, ss, rs, dev):
        return pltpu.make_async_remote_copy(
            src_ref=src, dst_ref=dst, send_sem=ss, recv_sem=rs, device_id=dev, device_id_type=MESH
        )

    halo = []
    for side, b in ((0, right), (1, left)):
        dev = {"blk": b}
        e2 = pl.ds(last - 1, 1) if side == 0 else pl.ds(1, 1)
        e1 = pl.ds(last, 1) if side == 0 else pl.ds(0, 1)
        d3 = pl.ds(0, 1) if side == 0 else pl.ds(layers + 3, 1)
        d2 = pl.ds(1, 1) if side == 0 else pl.ds(layers + 2, 1)
        d1 = pl.ds(0, 1) if side == 0 else pl.ds(layers + 1, 1)
        n = 6 * side
        halo.append([
            remote(now.at[0, :, e1], w0.at[:, d2, body], hsend.at[n], hrecv.at[n], dev),
            remote(mu.at[e1], md.at[1, d1], hsend.at[n + 1], hrecv.at[n + 1], dev),
            remote(lame.at[e1], md.at[0, d1], hsend.at[n + 2], hrecv.at[n + 2], dev),
            remote(now.at[0, :, e2], w0.at[:, d3, body], hsend.at[n + 3], hrecv.at[n + 3], dev),
            remote(fwd.at[0, 0, :, e1], fw.at[0, :, d1, body], hsend.at[n + 4], hrecv.at[n + 4], dev),
            remote(fwd.at[0, 1, :, e1], fw.at[1, :, d1, body], hsend.at[n + 5], hrecv.at[n + 5], dev),
        ])
    for j in range(3):
        halo[0][j].start()
        halo[1][j].start()
    edge_layer = pl.ds(last * tail, 1)
    inner_layer = pl.ds(1 + (last - 2) * tail, 1)
    handed = [
        remote(now.at[0, :, inner_layer], passed_now, psend.at[0], precv.at[0], {"blk": mirror})
    ] + [
        remote(
            fwd.at[0, j, :, edge_layer], passed.at[j], psend.at[j + 1], precv.at[j + 1],
            {"blk": mirror},
        )
        for j in range(2)
    ]
    far_layer = pl.ds((layers + 1) * tail, 1)
    onward = [
        remote(
            passed_now, w0.at[:, pl.ds((layers + 3) * tail, 1), body],
            fsend.at[0], hrecv.at[6 * tail + 3], {"blk": beyond},
        )
    ] + [
        remote(
            passed.at[j], fw.at[j, :, far_layer, body], fsend.at[j + 1],
            hrecv.at[6 * tail + 4 + j], {"blk": beyond},
        )
        for j in range(2)
    ]

    @pl.when(at_edge)
    def _():
        for c in handed:
            c.start()

    @pl.when(jnp.logical_not(is_tail))
    def _():
        for c in halo[0][3:]:
            c.start()

    @pl.when(jnp.logical_not(is_head))
    def _():
        for c in halo[1][3:]:
            c.start()

    for j in range(3, 7):
        loc[j].start()

    blank = jnp.zeros((PAD, 128), jnp.float32)
    for top in (0, PAD + height):
        edge = pl.ds(top, PAD)
        for b in range(3):
            for i in range(1, layers + 3):
                w0[b, i, edge, :] = blank
                w1[b, i, edge, :] = blank
            for i in range(1, layers + 1):
                fw[0, b, i, edge, :] = blank
                fw[1, b, i, edge, :] = blank
        for i in range(layers):
            s12[i + 1, edge, :] = blank
            s22[i, edge, :] = blank
            s23[i, edge, :] = blank

    lane = lax.broadcasted_iota(jnp.int32, (ROWS, 128), 1)
    first_lane = lane == 0
    last_lane = lane == 127

    def cross(c):
        return jnp.where(last_lane, 0.0, pltpu.roll(c, 127, 1)) - jnp.where(
            first_lane, 0.0, pltpu.roll(c, 1, 1)
        )

    def grads(u, i, r):
        here, up, down = pl.ds(PAD + r, ROWS), pl.ds(PAD + r + 1, ROWS), pl.ds(PAD + r - 1, ROWS)
        g1 = [u[b, i + 1, here, :] - u[b, i - 1, here, :] for b in range(3)]
        g2 = [u[b, i, up, :] - u[b, i, down, :] for b in range(3)]
        g3 = [cross(u[b, i, here, :]) for b in range(3)]
        return (
            g1[0], g2[1], g3[2], g1[1] + g2[0], g1[2] + g3[0], g2[2] + g3[1],
            g1[0] + g2[1] + g3[2],
        )

    def strain_pass(u, step, i, stress, place=None):
        for r in chunks:
            rows = pl.ds(r, ROWS)
            prow = pl.ds(PAD + r, ROWS)
            a, b, c, h12, h13, h23, tr = grads(u, i + 2, r)
            if stress:
                m = md[1, i + 1, rows, :]
                lt = md[0, i + 1, rows, :] * tr
                m2 = m + m
                s11[i + 1, rows, :] = m2 * a + lt
                s12[i + 1, prow, :] = m * h12
                s13[i + 1, rows, :] = m * h13
                if stress == 2:
                    s22[i, prow, :] = m2 * b + lt
                    s23[i, prow, :] = m * h23
                    s33[i, rows, :] = m2 * c + lt
            if place is not None:
                fa, fb, fc, f12, f13, f23, ft = grads(fw.at[step], i + 1, r)
                bulk = tr * ft
                con = (
                    (a * fa + b * fb + c * fc)
                    + 0.5 * (h12 * f12 + h13 * f13 + h23 * f23)
                    - bulk * (1.0 / 3.0)
                )
                d, q = r // band, pl.ds(r % band, ROWS)
                if step == 0:
                    part[d, place, 0, q, :] = con
                    part[d, place, 1, q, :] = bulk
                else:
                    part[d, place, 0, q, :] += con
                    part[d, place, 1, q, :] += bulk

    def update_pass(u, former, i, store):
        for r in chunks:
            rows = pl.ds(r, ROWS)
            here, up, down = pl.ds(PAD + r, ROWS), pl.ds(PAD + r + 1, ROWS), pl.ds(PAD + r - 1, ROWS)
            k = cf[i, rows, :]
            t1 = (
                (s11[i + 2, rows, :] - s11[i, rows, :])
                + (s12[i + 1, up, :] - s12[i + 1, down, :])
                + cross(s13[i + 1, rows, :])
            )
            t2 = (
                (s12[i + 2, here, :] - s12[i, here, :])
                + (s22[i, up, :] - s22[i, down, :])
                + cross(s23[i, here, :])
            )
            t3 = (
                (s13[i + 2, rows, :] - s13[i, rows, :])
                + (s23[i, up, :] - s23[i, down, :])
                + cross(s33[i, rows, :])
            )
            for b, t in enumerate((t1, t2, t3)):
                store(b, i, r, 2.0 * u[b, i + 2, here, :] - former(b, i, r) + k * t)

    def loop(low, high, f):
        def step(t, carry):
            f(t)
            return carry

        lax.fori_loop(low, high, step, 0)

    def first_former(b, i, r):
        return pv[b, i, pl.ds(r, ROWS), :]

    def first_store(b, i, r, value):
        w1[b, i + 2, pl.ds(PAD + r, ROWS), :] = value

    def first_update(i):
        update_pass(w0, first_former, i, first_store)

    def second_former(b, i, r):
        return w0[b, i + 2, pl.ds(PAD + r, ROWS), :]

    def second_store(b, i, r, value):
        res[b, i, pl.ds(r, ROWS), :] = value

    def second_update(i):
        update_pass(w1, second_former, i, second_store)

    sums = []

    def send_terms(group, low, count):
        for k in range(1, ne):
            dest = lax.rem(me_e + k, ne)
            n = group * ne + k
            sums.append(remote(
                part.at[dest, pl.ds(low, count)], got.at[k, pl.ds(low, count)],
                rsend.at[n], rrecv.at[n], {"event": dest},
            ))
            sums[-1].start()

    for j in range(4):
        loc[j].wait()
    loop(1, 3, lambda i: strain_pass(w0, 0, i, 2, i + 1))

    @pl.when(at_edge)
    def _():
        handed[0].wait_recv()
        onward[0].start()

    loop(3, 5, lambda i: strain_pass(w0, 0, i, 2, i - 3))
    loop(5, 7, lambda i: strain_pass(w0, 0, i, 2, i - 1))
    loc[4].wait()
    loc[5].wait()

    def coefficient(i):
        cf[i] = (0.25 * time_step * time_step) / cf[i]

    loop(0, layers, coefficient)
    loop(2, 6, first_update)

    @pl.when(at_edge)
    def _():
        for j in (1, 2):
            handed[j].wait_recv()
            onward[j].start()

    loc[6].wait()
    loop(3, 5, lambda i: strain_pass(w1, 1, i, 2, i - 3))
    send_terms(0, 0, 2)

    for side in (0, 1):
        for j in range(4):
            halo[side][j].wait_recv()
    loop(0, 2, lambda t: strain_pass(w0, 0, last * t, 2))
    loop(0, 2, lambda t: strain_pass(w0, 0, (layers + 1) * t - 1, 1))
    def edge_copy(source, target, n, b):
        return remote(
            w1.at[:, pl.ds(source, 1), body], w1.at[:, pl.ds(target, 1), body],
            usend.at[n], urecv.at[n], {"blk": b},
        )

    near = [edge_copy(layers + 1, 1, 0, right), edge_copy(2, layers + 2, 1, left)]
    far = [edge_copy(layers, 0, 2, right), edge_copy(3, layers + 3, 3, left)]
    loop(7, 8, first_update)
    near[0].start()
    loop(0, 1, first_update)
    near[1].start()
    loop(0, 2, lambda t: first_update(1 + 5 * t))
    far[0].start()
    far[1].start()

    loop(1, 3, lambda i: strain_pass(w1, 1, i, 2, i + 1))
    loop(5, 7, lambda i: strain_pass(w1, 1, i, 2, i - 1))
    send_terms(1, 2, 4)
    for side in (0, 1):
        halo[side][4].wait_recv()
    loop(0, 2, lambda t: strain_pass(w0, 0, last * t, 0, 6 + t))
    loop(2, 6, second_update)

    for c in near:
        c.wait_recv()
    for side in (0, 1):
        halo[side][5].wait_recv()
    loop(0, 2, lambda t: strain_pass(w1, 1, last * t, 2, 6 + t))
    send_terms(2, 6, 2)
    for c in far:
        c.wait_recv()
    loop(0, 2, lambda t: strain_pass(w1, 1, (layers + 1) * t - 1, 1))
    loop(0, 2, second_update)
    loop(6, 8, second_update)

    mine = pl.ds(pl.multiple_of(me_e * band, band), band)
    for c in sums:
        c.wait_recv()
    for p, i in enumerate((3, 4, 1, 2, 5, 6, 0, 7)):
        con = part[me_e, p, 0]
        bulk = part[me_e, p, 1]
        for k in range(1, ne):
            con = con + got[k, p, 0]
            bulk = bulk + got[k, p, 1]
        m = md[1, i + 1, mine, :]
        sh[i] = (-0.5 * time_step) * m * con
        bk[i] = (-0.25 * time_step) * (md[0, i + 1, mine, :] + (2.0 / 3.0) * m) * bulk

    for side in (0, 1):
        for c in halo[side][:3]:
            c.wait_send()

    @pl.when(at_edge)
    def _():
        for c in handed + onward:
            c.wait_send()

    @pl.when(jnp.logical_not(is_tail))
    def _():
        for c in halo[0][3:]:
            c.wait_send()

    @pl.when(jnp.logical_not(is_head))
    def _():
        for c in halo[1][3:]:
            c.wait_send()

    for c in near + far:
        c.wait_send()
    for c in sums:
        c.wait_send()


def put_out(field, shear, bulk, field_out, shear_out, bulk_out, sem):
    copies = [
        pltpu.make_async_copy(field, field_out.at[0], sem.at[0]),
        pltpu.make_async_copy(shear, shear_out, sem.at[1]),
        pltpu.make_async_copy(bulk, bulk_out, sem.at[2]),
    ]
    for c in copies:
        c.start()
    for c in copies:
        c.wait()


def local(nb, ne, adjoint_now, adjoint_prev, forward_field, density, lame_first, shear_modulus):
    layers, height, width = density.shape
    tall = height + 2 * PAD
    band = height // ne
    run = 16 if nb % 16 == 0 else 2
    f32 = jnp.float32
    dma = pltpu.SemaphoreType.DMA
    anywhere = pl.BlockSpec(memory_space=pl.ANY)
    vmem = pl.BlockSpec(memory_space=pltpu.VMEM)
    results = pl.pallas_call(
        functools.partial(kernel, nb, ne, run),
        out_shape=(
            pltpu.VMEM((3, layers, height, width), f32),
            pltpu.VMEM((layers, band, width), f32),
            pltpu.VMEM((layers, band, width), f32),
        ),
        in_specs=[anywhere] * 6,
        out_specs=(vmem,) * 3,
        scratch_shapes=[
            pltpu.VMEM((3, layers + 4, tall, width), f32),
            pltpu.VMEM((3, layers + 4, tall, width), f32),
            pltpu.VMEM((3, layers, height, width), f32),
            pltpu.VMEM((2, 3, layers + 2, tall, width), f32),
            pltpu.VMEM((2, layers + 2, height, width), f32),
            pltpu.VMEM((layers, height, width), f32),
            pltpu.VMEM((layers + 2, height, width), f32),
            pltpu.VMEM((layers + 2, tall, width), f32),
            pltpu.VMEM((layers + 2, height, width), f32),
            pltpu.VMEM((layers, tall, width), f32),
            pltpu.VMEM((layers, tall, width), f32),
            pltpu.VMEM((layers, height, width), f32),
            pltpu.VMEM((ne, layers, 2, band, width), f32),
            pltpu.VMEM((ne, layers, 2, band, width), f32),
            pltpu.VMEM((2, 3, 1, height, width), f32),
            pltpu.VMEM((3, 1, height, width), f32),
            dma((7,)),
            dma((12,)),
            dma((12,)),
            dma((4,)),
            dma((4,)),
            dma((3 * ne,)),
            dma((3 * ne,)),
            dma((3,)),
            dma((3,)),
            dma((3,)),
        ],
        compiler_params=pltpu.CompilerParams(collective_id=0, has_side_effects=True),
        name="adjoint",
    )(adjoint_now, adjoint_prev, forward_field, density, lame_first, shear_modulus)
    return pl.pallas_call(
        put_out,
        out_shape=(
            jax.ShapeDtypeStruct((1, 3, layers, height, width), f32),
            jax.ShapeDtypeStruct((layers, band, width), f32),
            jax.ShapeDtypeStruct((layers, band, width), f32),
        ),
        in_specs=[anywhere] * 3,
        out_specs=(anywhere,) * 3,
        scratch_shapes=[dma((3,))],
        compiler_params=pltpu.CompilerParams(vmem_limit_bytes=1 << 20),
        name="put_out",
    )(*results)


def solution(mesh):
    in_specs = (
        P("event", None, "blk", None, None),
        P("event", None, "blk", None, None),
        P("event", None, None, "blk", None, None),
        P("blk", None, None),
        P("blk", None, None),
        P("blk", None, None),
    )
    out_specs = (
        P("event", None, "blk", None, None),
        P("blk", "event", None),
        P("blk", "event", None),
    )
    body = functools.partial(local, mesh.shape["blk"], mesh.shape["event"])
    return jax.shard_map(body, mesh=mesh, in_specs=in_specs, out_specs=out_specs, check_vma=False)
```

```python
import functools

import jax
import jax.numpy as jnp
from jax import lax
from jax.experimental import pallas as pl
from jax.experimental.pallas import tpu as pltpu
from jax.sharding import PartitionSpec as P

MESH = pl.DeviceIdType.MESH
time_step = 0.3
PAD = 8
ROWS = 8


def kernel(
    nb, ne, run, now, prev, fwd, dens, lame, mu, res, sh, bk,
    w0, w1, pv, fw, md, cf, s11, s12, s13, s22, s23, s33, part, got, passed, passed_now,
    lsem, hsend, hrecv, usend, urecv, rsend, rrecv, psend, precv, fsend,
):
    layers, height = dens.shape[0], dens.shape[1]
    last = layers - 1
    band = height // ne
    me_b = lax.axis_index("blk")
    me_e = lax.axis_index("event")
    right = lax.rem(me_b + 1, nb)
    left = lax.rem(me_b + nb - 1, nb)
    body = pl.ds(PAD, height)

    spot = lax.rem(me_b, run)
    is_head = spot == 0
    is_tail = spot == run - 1
    at_edge = jnp.logical_or(is_head, is_tail)
    tail = lax.div(spot, run - 1)
    mirror = me_b - spot + (run - 1 - spot)
    beyond = lax.rem(me_b + run * (1 - 2 * tail) + nb, nb)
    chunks = range(0, height, ROWS)

    barrier = pltpu.get_barrier_semaphore()
    for b in (left, right, mirror, lax.rem(me_b + run, nb), lax.rem(me_b + nb - run, nb)):
        pl.semaphore_signal(barrier, inc=1, device_id={"blk": b}, device_id_type=MESH)
    for k in range(1, ne):
        pl.semaphore_signal(
            barrier, inc=1, device_id={"event": lax.rem(me_e + k, ne)}, device_id_type=MESH
        )

    own = pl.ds(1, layers)
    loc = [
        pltpu.make_async_copy(now.at[0], w0.at[:, pl.ds(2, layers), body], lsem.at[0]),
        pltpu.make_async_copy(mu, md.at[1, own], lsem.at[1]),
        pltpu.make_async_copy(lame, md.at[0, own], lsem.at[2]),
        pltpu.make_async_copy(fwd.at[0, 0], fw.at[0, :, own, body], lsem.at[3]),
        pltpu.make_async_copy(dens, cf, lsem.at[4]),
        pltpu.make_async_copy(prev.at[0], pv, lsem.at[5]),
        pltpu.make_async_copy(fwd.at[0, 1], fw.at[1, :, own, body], lsem.at[6]),
    ]
    for j in range(3):
        loc[j].start()

    pl.semaphore_wait(barrier, ne + 4)

    def remote(src, dst, ss, rs, dev):
        return pltpu.make_async_remote_copy(
            src_ref=src, dst_ref=dst, send_sem=ss, recv_sem=rs, device_id=dev, device_id_type=MESH
        )

    halo = []
    for side, b in ((0, right), (1, left)):
        dev = {"blk": b}
        e2 = pl.ds(last - 1, 1) if side == 0 else pl.ds(1, 1)
        e1 = pl.ds(last, 1) if side == 0 else pl.ds(0, 1)
        d3 = pl.ds(0, 1) if side == 0 else pl.ds(layers + 3, 1)
        d2 = pl.ds(1, 1) if side == 0 else pl.ds(layers + 2, 1)
        d1 = pl.ds(0, 1) if side == 0 else pl.ds(layers + 1, 1)
        n = 6 * side
        halo.append([
            remote(now.at[0, :, e1], w0.at[:, d2, body], hsend.at[n], hrecv.at[n], dev),
            remote(mu.at[e1], md.at[1, d1], hsend.at[n + 1], hrecv.at[n + 1], dev),
            remote(lame.at[e1], md.at[0, d1], hsend.at[n + 2], hrecv.at[n + 2], dev),
            remote(now.at[0, :, e2], w0.at[:, d3, body], hsend.at[n + 3], hrecv.at[n + 3], dev),
            remote(fwd.at[0, 0, :, e1], fw.at[0, :, d1, body], hsend.at[n + 4], hrecv.at[n + 4], dev),
            remote(fwd.at[0, 1, :, e1], fw.at[1, :, d1, body], hsend.at[n + 5], hrecv.at[n + 5], dev),
        ])
    for j in range(3):
        halo[0][j].start()
        halo[1][j].start()
    edge_layer = pl.ds(last * tail, 1)
    inner_layer = pl.ds(1 + (last - 2) * tail, 1)
    handed = [
        remote(now.at[0, :, inner_layer], passed_now, psend.at[0], precv.at[0], {"blk": mirror})
    ] + [
        remote(
            fwd.at[0, j, :, edge_layer], passed.at[j], psend.at[j + 1], precv.at[j + 1],
            {"blk": mirror},
        )
        for j in range(2)
    ]
    far_layer = pl.ds((layers + 1) * tail, 1)
    onward = [
        remote(
            passed_now, w0.at[:, pl.ds((layers + 3) * tail, 1), body],
            fsend.at[0], hrecv.at[6 * tail + 3], {"blk": beyond},
        )
    ] + [
        remote(
            passed.at[j], fw.at[j, :, far_layer, body], fsend.at[j + 1],
            hrecv.at[6 * tail + 4 + j], {"blk": beyond},
        )
        for j in range(2)
    ]

    @pl.when(at_edge)
    def _():
        for c in handed:
            c.start()

    @pl.when(jnp.logical_not(is_tail))
    def _():
        for c in halo[0][3:]:
            c.start()

    @pl.when(jnp.logical_not(is_head))
    def _():
        for c in halo[1][3:]:
            c.start()

    for j in range(3, 7):
        loc[j].start()

    blank = jnp.zeros((PAD, 128), jnp.float32)
    for top in (0, PAD + height):
        edge = pl.ds(top, PAD)
        for b in range(3):
            for i in range(1, layers + 3):
                w0[b, i, edge, :] = blank
                w1[b, i, edge, :] = blank
            for i in range(1, layers + 1):
                fw[0, b, i, edge, :] = blank
                fw[1, b, i, edge, :] = blank
        for i in range(layers):
            s12[i + 1, edge, :] = blank
            s22[i, edge, :] = blank
            s23[i, edge, :] = blank

    lane = lax.broadcasted_iota(jnp.int32, (ROWS, 128), 1)
    first_lane = lane == 0
    last_lane = lane == 127

    def cross(c):
        return jnp.where(last_lane, 0.0, pltpu.roll(c, 127, 1)) - jnp.where(
            first_lane, 0.0, pltpu.roll(c, 1, 1)
        )

    def grads(u, i, r):
        here, up, down = pl.ds(PAD + r, ROWS), pl.ds(PAD + r + 1, ROWS), pl.ds(PAD + r - 1, ROWS)
        g1 = [u[b, i + 1, here, :] - u[b, i - 1, here, :] for b in range(3)]
        g2 = [u[b, i, up, :] - u[b, i, down, :] for b in range(3)]
        g3 = [cross(u[b, i, here, :]) for b in range(3)]
        return (
            g1[0], g2[1], g3[2], g1[1] + g2[0], g1[2] + g3[0], g2[2] + g3[1],
            g1[0] + g2[1] + g3[2],
        )

    def strain_pass(u, step, i, stress, place=None):
        for r in chunks:
            rows = pl.ds(r, ROWS)
            prow = pl.ds(PAD + r, ROWS)
            a, b, c, h12, h13, h23, tr = grads(u, i + 2, r)
            if stress:
                m = md[1, i + 1, rows, :]
                lt = md[0, i + 1, rows, :] * tr
                m2 = m + m
                s11[i + 1, rows, :] = m2 * a + lt
                s12[i + 1, prow, :] = m * h12
                s13[i + 1, rows, :] = m * h13
                if stress == 2:
                    s22[i, prow, :] = m2 * b + lt
                    s23[i, prow, :] = m * h23
                    s33[i, rows, :] = m2 * c + lt
            if place is not None:
                fa, fb, fc, f12, f13, f23, ft = grads(fw.at[step], i + 1, r)
                bulk = tr * ft
                con = (
                    (a * fa + b * fb + c * fc)
                    + 0.5 * (h12 * f12 + h13 * f13 + h23 * f23)
                    - bulk * (1.0 / 3.0)
                )
                d, q = r // band, pl.ds(r % band, ROWS)
                if step == 0:
                    part[d, place, 0, q, :] = con
                    part[d, place, 1, q, :] = bulk
                else:
                    part[d, place, 0, q, :] += con
                    part[d, place, 1, q, :] += bulk

    def update_pass(u, former, i, store):
        for r in chunks:
            rows = pl.ds(r, ROWS)
            here, up, down = pl.ds(PAD + r, ROWS), pl.ds(PAD + r + 1, ROWS), pl.ds(PAD + r - 1, ROWS)
            k = cf[i, rows, :]
            t1 = (
                (s11[i + 2, rows, :] - s11[i, rows, :])
                + (s12[i + 1, up, :] - s12[i + 1, down, :])
                + cross(s13[i + 1, rows, :])
            )
            t2 = (
                (s12[i + 2, here, :] - s12[i, here, :])
                + (s22[i, up, :] - s22[i, down, :])
                + cross(s23[i, here, :])
            )
            t3 = (
                (s13[i + 2, rows, :] - s13[i, rows, :])
                + (s23[i, up, :] - s23[i, down, :])
                + cross(s33[i, rows, :])
            )
            for b, t in enumerate((t1, t2, t3)):
                store(b, i, r, 2.0 * u[b, i + 2, here, :] - former(b, i, r) + k * t)

    def loop(low, high, f):
        def step(t, carry):
            f(t)
            return carry

        lax.fori_loop(low, high, step, 0)

    def first_former(b, i, r):
        return pv[b, i, pl.ds(r, ROWS), :]

    def first_store(b, i, r, value):
        w1[b, i + 2, pl.ds(PAD + r, ROWS), :] = value

    def first_update(i):
        update_pass(w0, first_former, i, first_store)

    def second_former(b, i, r):
        return w0[b, i + 2, pl.ds(PAD + r, ROWS), :]

    def second_store(b, i, r, value):
        res[b, i, pl.ds(r, ROWS), :] = value

    def second_update(i):
        update_pass(w1, second_former, i, second_store)

    sums = []

    def send_terms(group, low, count):
        for k in range(1, ne):
            dest = lax.rem(me_e + k, ne)
            n = group * ne + k
            sums.append(remote(
                part.at[dest, pl.ds(low, count)], got.at[k, pl.ds(low, count)],
                rsend.at[n], rrecv.at[n], {"event": dest},
            ))
            sums[-1].start()

    for j in range(4):
        loc[j].wait()
    loop(1, 3, lambda i: strain_pass(w0, 0, i, 2, i + 1))

    @pl.when(at_edge)
    def _():
        handed[0].wait_recv()
        onward[0].start()

    loop(3, 5, lambda i: strain_pass(w0, 0, i, 2, i - 3))
    loop(5, 7, lambda i: strain_pass(w0, 0, i, 2, i - 1))
    loc[4].wait()
    loc[5].wait()

    def coefficient(i):
        cf[i] = (0.25 * time_step * time_step) / cf[i]

    loop(0, layers, coefficient)
    loop(2, 6, first_update)

    @pl.when(at_edge)
    def _():
        for j in (1, 2):
            handed[j].wait_recv()
            onward[j].start()

    loc[6].wait()
    loop(3, 5, lambda i: strain_pass(w1, 1, i, 2, i - 3))
    send_terms(0, 0, 2)

    early = is_head.astype(jnp.int32)

    def face(n):
        return early + n * (1 - 2 * early)

    def arrival(side, j):
        d1 = pl.ds((layers + 1) * side, 1)
        sem = hrecv.at[6 * side + j]
        if j == 0:
            dst = w0.at[:, pl.ds(1 + (layers + 1) * side, 1), body]
        elif j == 3:
            dst = w0.at[:, pl.ds((layers + 3) * side, 1), body]
        elif j in (1, 2):
            dst = md.at[2 - j, d1]
        else:
            dst = fw.at[j - 4, :, d1, body]
        return remote(dst, dst, hsend.at[6 * side + j], sem, {"blk": left})

    def edge_copy(source, target, n, b):
        return remote(
            w1.at[:, pl.ds(source, 1), body], w1.at[:, pl.ds(target, 1), body],
            usend.at[n], urecv.at[n], {"blk": b},
        )

    def edge_copies(side):
        b = lax.rem(me_b + nb + 2 * side - 1, nb)
        there = 1 - side
        return (
            edge_copy(2 + last * side, 1 + (layers + 1) * there, there, b),
            edge_copy(3 + (last - 2) * side, (layers + 3) * there, 2 + there, b),
        )

    def first_edge(n):
        side = face(n)
        for j in range(4):
            arrival(side, j).wait_recv()
        strain_pass(w0, 0, last * side, 2)
        strain_pass(w0, 0, (layers + 1) * side - 1, 1)
        near, far = edge_copies(side)
        first_update(last * side)
        near.start()
        first_update(1 + (last - 2) * side)
        far.start()

    loop(0, 2, first_edge)

    loop(1, 3, lambda i: strain_pass(w1, 1, i, 2, i + 1))
    loop(5, 7, lambda i: strain_pass(w1, 1, i, 2, i - 1))
    send_terms(1, 2, 4)
    loop(2, 6, second_update)

    def forward_edge(n):
        side = face(n)
        arrival(side, 4).wait_recv()
        strain_pass(w0, 0, last * side, 0, 6 + side)

    loop(0, 2, forward_edge)

    def terms_copy(side, k):
        dest = lax.rem(me_e + k, ne)
        m = (2 + side) * ne + k
        return remote(
            part.at[dest, pl.ds(6 + side, 1)], got.at[k, pl.ds(6 + side, 1)],
            rsend.at[m], rrecv.at[m], {"event": dest},
        )

    def second_edge(n):
        side = face(n)
        edge_copy(2, 1 + (layers + 1) * side, side, left).wait_recv()
        arrival(side, 5).wait_recv()
        strain_pass(w1, 1, last * side, 2, 6 + side)
        for k in range(1, ne):
            terms_copy(side, k).start()

    loop(0, 2, second_edge)
    for side in (0, 1):
        for k in range(1, ne):
            sums.append(terms_copy(side, k))
    for side in (0, 1):
        edge_copy(2, (layers + 3) * side, 2 + side, left).wait_recv()
    loop(0, 2, lambda t: strain_pass(w1, 1, (layers + 1) * t - 1, 1))
    loop(0, 2, second_update)
    loop(6, 8, second_update)

    mine = pl.ds(pl.multiple_of(me_e * band, band), band)
    for c in sums:
        c.wait_recv()
    for p, i in enumerate((3, 4, 1, 2, 5, 6, 0, 7)):
        con = part[me_e, p, 0]
        bulk = part[me_e, p, 1]
        for k in range(1, ne):
            con = con + got[k, p, 0]
            bulk = bulk + got[k, p, 1]
        m = md[1, i + 1, mine, :]
        sh[i] = (-0.5 * time_step) * m * con
        bk[i] = (-0.25 * time_step) * (md[0, i + 1, mine, :] + (2.0 / 3.0) * m) * bulk

    for side in (0, 1):
        for c in halo[side][:3]:
            c.wait_send()

    @pl.when(at_edge)
    def _():
        for c in handed + onward:
            c.wait_send()

    @pl.when(jnp.logical_not(is_tail))
    def _():
        for c in halo[0][3:]:
            c.wait_send()

    @pl.when(jnp.logical_not(is_head))
    def _():
        for c in halo[1][3:]:
            c.wait_send()

    for side in (0, 1):
        for c in edge_copies(side):
            c.wait_send()
    for c in sums:
        c.wait_send()


def put_out(field, shear, bulk, field_out, shear_out, bulk_out, sem):
    copies = [
        pltpu.make_async_copy(field, field_out.at[0], sem.at[0]),
        pltpu.make_async_copy(shear, shear_out, sem.at[1]),
        pltpu.make_async_copy(bulk, bulk_out, sem.at[2]),
    ]
    for c in copies:
        c.start()
    for c in copies:
        c.wait()


def local(nb, ne, adjoint_now, adjoint_prev, forward_field, density, lame_first, shear_modulus):
    layers, height, width = density.shape
    tall = height + 2 * PAD
    band = height // ne
    run = 16 if nb % 16 == 0 else 2
    f32 = jnp.float32
    dma = pltpu.SemaphoreType.DMA
    anywhere = pl.BlockSpec(memory_space=pl.ANY)
    vmem = pl.BlockSpec(memory_space=pltpu.VMEM)
    results = pl.pallas_call(
        functools.partial(kernel, nb, ne, run),
        out_shape=(
            pltpu.VMEM((3, layers, height, width), f32),
            pltpu.VMEM((layers, band, width), f32),
            pltpu.VMEM((layers, band, width), f32),
        ),
        in_specs=[anywhere] * 6,
        out_specs=(vmem,) * 3,
        scratch_shapes=[
            pltpu.VMEM((3, layers + 4, tall, width), f32),
            pltpu.VMEM((3, layers + 4, tall, width), f32),
            pltpu.VMEM((3, layers, height, width), f32),
            pltpu.VMEM((2, 3, layers + 2, tall, width), f32),
            pltpu.VMEM((2, layers + 2, height, width), f32),
            pltpu.VMEM((layers, height, width), f32),
            pltpu.VMEM((layers + 2, height, width), f32),
            pltpu.VMEM((layers + 2, tall, width), f32),
            pltpu.VMEM((layers + 2, height, width), f32),
            pltpu.VMEM((layers, tall, width), f32),
            pltpu.VMEM((layers, tall, width), f32),
            pltpu.VMEM((layers, height, width), f32),
            pltpu.VMEM((ne, layers, 2, band, width), f32),
            pltpu.VMEM((ne, layers, 2, band, width), f32),
            pltpu.VMEM((2, 3, 1, height, width), f32),
            pltpu.VMEM((3, 1, height, width), f32),
            dma((7,)),
            dma((12,)),
            dma((12,)),
            dma((4,)),
            dma((4,)),
            dma((4 * ne,)),
            dma((4 * ne,)),
            dma((3,)),
            dma((3,)),
            dma((3,)),
        ],
        compiler_params=pltpu.CompilerParams(collective_id=0, has_side_effects=True),
        name="adjoint",
    )(adjoint_now, adjoint_prev, forward_field, density, lame_first, shear_modulus)
    return pl.pallas_call(
        put_out,
        out_shape=(
            jax.ShapeDtypeStruct((1, 3, layers, height, width), f32),
            jax.ShapeDtypeStruct((layers, band, width), f32),
            jax.ShapeDtypeStruct((layers, band, width), f32),
        ),
        in_specs=[anywhere] * 3,
        out_specs=(anywhere,) * 3,
        scratch_shapes=[dma((3,))],
        compiler_params=pltpu.CompilerParams(vmem_limit_bytes=1 << 20),
        name="put_out",
    )(*results)


def solution(mesh):
    in_specs = (
        P("event", None, "blk", None, None),
        P("event", None, "blk", None, None),
        P("event", None, None, "blk", None, None),
        P("blk", None, None),
        P("blk", None, None),
        P("blk", None, None),
    )
    out_specs = (
        P("event", None, "blk", None, None),
        P("blk", "event", None),
        P("blk", "event", None),
    )
    body = functools.partial(local, mesh.shape["blk"], mesh.shape["event"])
    return jax.shard_map(body, mesh=mesh, in_specs=in_specs, out_specs=out_specs, check_vma=False)
```

```python
import functools

import jax
import jax.numpy as jnp
from jax import lax
from jax.experimental import pallas as pl
from jax.experimental.pallas import tpu as pltpu
from jax.sharding import PartitionSpec as P

MESH = pl.DeviceIdType.MESH
time_step = 0.3
PAD = 8
ROWS = 8


def kernel(
    nb, ne, run, now, prev, fwd, dens, lame, mu, res, sh, bk,
    w0, w1, pv, fw, md, cf, s11, s12, s13, s22, s23, s33, part, got, passed, passed_now,
    lsem, hsend, hrecv, usend, urecv, rsend, rrecv, psend, precv, fsend,
):
    layers, height = dens.shape[0], dens.shape[1]
    last = layers - 1
    band = height // ne
    me_b = lax.axis_index("blk")
    me_e = lax.axis_index("event")
    right = lax.rem(me_b + 1, nb)
    left = lax.rem(me_b + nb - 1, nb)
    body = pl.ds(PAD, height)

    spot = lax.rem(me_b, run)
    is_head = spot == 0
    is_tail = spot == run - 1
    at_edge = jnp.logical_or(is_head, is_tail)
    tail = lax.div(spot, run - 1)
    mirror = me_b - spot + (run - 1 - spot)
    beyond = lax.rem(me_b + run * (1 - 2 * tail) + nb, nb)
    chunks = range(0, height, ROWS)

    barrier = pltpu.get_barrier_semaphore()
    for b in (left, right, mirror, lax.rem(me_b + run, nb), lax.rem(me_b + nb - run, nb)):
        pl.semaphore_signal(barrier, inc=1, device_id={"blk": b}, device_id_type=MESH)
    for k in range(1, ne):
        pl.semaphore_signal(
            barrier, inc=1, device_id={"event": lax.rem(me_e + k, ne)}, device_id_type=MESH
        )

    own = pl.ds(1, layers)
    loc = [
        pltpu.make_async_copy(now.at[0], w0.at[:, pl.ds(2, layers), body], lsem.at[0]),
        pltpu.make_async_copy(mu, md.at[1, own], lsem.at[1]),
        pltpu.make_async_copy(lame, md.at[0, own], lsem.at[2]),
        pltpu.make_async_copy(fwd.at[0, 0], fw.at[0, :, own, body], lsem.at[3]),
        pltpu.make_async_copy(dens, cf, lsem.at[4]),
        pltpu.make_async_copy(prev.at[0], pv, lsem.at[5]),
        pltpu.make_async_copy(fwd.at[0, 1], fw.at[1, :, own, body], lsem.at[6]),
    ]
    for j in range(3):
        loc[j].start()

    pl.semaphore_wait(barrier, ne + 4)

    def remote(src, dst, ss, rs, dev):
        return pltpu.make_async_remote_copy(
            src_ref=src, dst_ref=dst, send_sem=ss, recv_sem=rs, device_id=dev, device_id_type=MESH
        )

    halo = []
    for side, b in ((0, right), (1, left)):
        dev = {"blk": b}
        e2 = pl.ds(last - 1, 1) if side == 0 else pl.ds(1, 1)
        e1 = pl.ds(last, 1) if side == 0 else pl.ds(0, 1)
        d3 = pl.ds(0, 1) if side == 0 else pl.ds(layers + 3, 1)
        d2 = pl.ds(1, 1) if side == 0 else pl.ds(layers + 2, 1)
        d1 = pl.ds(0, 1) if side == 0 else pl.ds(layers + 1, 1)
        n = 6 * side
        halo.append([
            remote(now.at[0, :, e1], w0.at[:, d2, body], hsend.at[n], hrecv.at[n], dev),
            remote(mu.at[e1], md.at[1, d1], hsend.at[n + 1], hrecv.at[n + 1], dev),
            remote(lame.at[e1], md.at[0, d1], hsend.at[n + 2], hrecv.at[n + 2], dev),
            remote(now.at[0, :, e2], w0.at[:, d3, body], hsend.at[n + 3], hrecv.at[n + 3], dev),
            remote(fwd.at[0, 0, :, e1], fw.at[0, :, d1, body], hsend.at[n + 4], hrecv.at[n + 4], dev),
            remote(fwd.at[0, 1, :, e1], fw.at[1, :, d1, body], hsend.at[n + 5], hrecv.at[n + 5], dev),
        ])
    for j in range(3):
        halo[0][j].start()
        halo[1][j].start()
    edge_layer = pl.ds(last * tail, 1)
    inner_layer = pl.ds(1 + (last - 2) * tail, 1)
    handed = [
        remote(now.at[0, :, inner_layer], passed_now, psend.at[0], precv.at[0], {"blk": mirror})
    ] + [
        remote(
            fwd.at[0, j, :, edge_layer], passed.at[j], psend.at[j + 1], precv.at[j + 1],
            {"blk": mirror},
        )
        for j in range(2)
    ]
    far_layer = pl.ds((layers + 1) * tail, 1)
    onward = [
        remote(
            passed_now, w0.at[:, pl.ds((layers + 3) * tail, 1), body],
            fsend.at[0], hrecv.at[6 * tail + 3], {"blk": beyond},
        )
    ] + [
        remote(
            passed.at[j], fw.at[j, :, far_layer, body], fsend.at[j + 1],
            hrecv.at[6 * tail + 4 + j], {"blk": beyond},
        )
        for j in range(2)
    ]

    @pl.when(at_edge)
    def _():
        for c in handed:
            c.start()

    @pl.when(jnp.logical_not(is_tail))
    def _():
        for c in halo[0][3:]:
            c.start()

    @pl.when(jnp.logical_not(is_head))
    def _():
        for c in halo[1][3:]:
            c.start()

    for j in range(3, 7):
        loc[j].start()

    blank = jnp.zeros((PAD, 128), jnp.float32)
    for top in (0, PAD + height):
        edge = pl.ds(top, PAD)
        for b in range(3):
            for i in range(1, layers + 3):
                w0[b, i, edge, :] = blank
                w1[b, i, edge, :] = blank
            for i in range(1, layers + 1):
                fw[0, b, i, edge, :] = blank
                fw[1, b, i, edge, :] = blank
        for i in range(layers):
            s12[i + 1, edge, :] = blank
            s22[i, edge, :] = blank
            s23[i, edge, :] = blank

    lane = lax.broadcasted_iota(jnp.int32, (ROWS, 128), 1)
    first_lane = lane == 0
    last_lane = lane == 127

    def cross(c):
        return jnp.where(last_lane, 0.0, pltpu.roll(c, 127, 1)) - jnp.where(
            first_lane, 0.0, pltpu.roll(c, 1, 1)
        )

    def grads(u, i, r):
        here, up, down = pl.ds(PAD + r, ROWS), pl.ds(PAD + r + 1, ROWS), pl.ds(PAD + r - 1, ROWS)
        g1 = [u[b, i + 1, here, :] - u[b, i - 1, here, :] for b in range(3)]
        g2 = [u[b, i, up, :] - u[b, i, down, :] for b in range(3)]
        g3 = [cross(u[b, i, here, :]) for b in range(3)]
        return (
            g1[0], g2[1], g3[2], g1[1] + g2[0], g1[2] + g3[0], g2[2] + g3[1],
            g1[0] + g2[1] + g3[2],
        )

    def strain_pass(u, step, i, stress, place=None):
        for r in chunks:
            rows = pl.ds(r, ROWS)
            prow = pl.ds(PAD + r, ROWS)
            a, b, c, h12, h13, h23, tr = grads(u, i + 2, r)
            if stress:
                m = md[1, i + 1, rows, :]
                lt = md[0, i + 1, rows, :] * tr
                m2 = m + m
                s11[i + 1, rows, :] = m2 * a + lt
                s12[i + 1, prow, :] = m * h12
                s13[i + 1, rows, :] = m * h13
                if stress == 2:
                    s22[i, prow, :] = m2 * b + lt
                    s23[i, prow, :] = m * h23
                    s33[i, rows, :] = m2 * c + lt
            if place is not None:
                fa, fb, fc, f12, f13, f23, ft = grads(fw.at[step], i + 1, r)
                bulk = tr * ft
                con = (
                    (a * fa + b * fb + c * fc)
                    + 0.5 * (h12 * f12 + h13 * f13 + h23 * f23)
                    - bulk * (1.0 / 3.0)
                )
                d, q = r // band, pl.ds(r % band, ROWS)
                if step == 0:
                    part[d, place, 0, q, :] = con
                    part[d, place, 1, q, :] = bulk
                else:
                    part[d, place, 0, q, :] += con
                    part[d, place, 1, q, :] += bulk

    def update_pass(u, former, i, store):
        for r in chunks:
            rows = pl.ds(r, ROWS)
            here, up, down = pl.ds(PAD + r, ROWS), pl.ds(PAD + r + 1, ROWS), pl.ds(PAD + r - 1, ROWS)
            k = cf[i, rows, :]
            t1 = (
                (s11[i + 2, rows, :] - s11[i, rows, :])
                + (s12[i + 1, up, :] - s12[i + 1, down, :])
                + cross(s13[i + 1, rows, :])
            )
            t2 = (
                (s12[i + 2, here, :] - s12[i, here, :])
                + (s22[i, up, :] - s22[i, down, :])
                + cross(s23[i, here, :])
            )
            t3 = (
                (s13[i + 2, rows, :] - s13[i, rows, :])
                + (s23[i, up, :] - s23[i, down, :])
                + cross(s33[i, rows, :])
            )
            for b, t in enumerate((t1, t2, t3)):
                store(b, i, r, 2.0 * u[b, i + 2, here, :] - former(b, i, r) + k * t)

    def loop(low, high, f):
        def step(t, carry):
            f(t)
            return carry

        lax.fori_loop(low, high, step, 0)

    def first_former(b, i, r):
        return pv[b, i, pl.ds(r, ROWS), :]

    def first_store(b, i, r, value):
        w1[b, i + 2, pl.ds(PAD + r, ROWS), :] = value

    def first_update(i):
        update_pass(w0, first_former, i, first_store)

    def second_former(b, i, r):
        return w0[b, i + 2, pl.ds(PAD + r, ROWS), :]

    def second_store(b, i, r, value):
        res[b, i, pl.ds(r, ROWS), :] = value

    def second_update(i):
        update_pass(w1, second_former, i, second_store)

    sums = []

    def send_terms(group, low, count):
        for k in range(1, ne):
            dest = lax.rem(me_e + k, ne)
            n = group * ne + k
            sums.append(remote(
                part.at[dest, pl.ds(low, count)], got.at[k, pl.ds(low, count)],
                rsend.at[n], rrecv.at[n], {"event": dest},
            ))
            sums[-1].start()

    for j in range(4):
        loc[j].wait()
    loop(1, 3, lambda i: strain_pass(w0, 0, i, 2, i + 1))

    @pl.when(at_edge)
    def _():
        handed[0].wait_recv()
        onward[0].start()

    loop(3, 5, lambda i: strain_pass(w0, 0, i, 2, i - 3))
    loop(5, 7, lambda i: strain_pass(w0, 0, i, 2, i - 1))
    loc[4].wait()
    loc[5].wait()

    def coefficient(i):
        cf[i] = (0.25 * time_step * time_step) / cf[i]

    loop(0, layers, coefficient)
    loop(2, 6, first_update)

    @pl.when(at_edge)
    def _():
        for j in (1, 2):
            handed[j].wait_recv()
            onward[j].start()

    loc[6].wait()
    loop(3, 5, lambda i: strain_pass(w1, 1, i, 2, i - 3))
    send_terms(0, 0, 2)

    early = is_head.astype(jnp.int32)

    def face(n):
        return early + n * (1 - 2 * early)

    def arrival(side, j):
        d1 = pl.ds((layers + 1) * side, 1)
        sem = hrecv.at[6 * side + j]
        if j == 0:
            dst = w0.at[:, pl.ds(1 + (layers + 1) * side, 1), body]
        elif j == 3:
            dst = w0.at[:, pl.ds((layers + 3) * side, 1), body]
        elif j in (1, 2):
            dst = md.at[2 - j, d1]
        else:
            dst = fw.at[j - 4, :, d1, body]
        return remote(dst, dst, hsend.at[6 * side + j], sem, {"blk": left})

    def edge_copy(source, target, n, b):
        return remote(
            w1.at[:, pl.ds(source, 1), body], w1.at[:, pl.ds(target, 1), body],
            usend.at[n], urecv.at[n], {"blk": b},
        )

    def edge_copies(side):
        b = lax.rem(me_b + nb + 2 * side - 1, nb)
        there = 1 - side
        return (
            edge_copy(2 + last * side, 1 + (layers + 1) * there, there, b),
            edge_copy(3 + (last - 2) * side, (layers + 3) * there, 2 + there, b),
        )

    def first_edge(n):
        side = face(n)
        for j in range(4):
            arrival(side, j).wait_recv()
        strain_pass(w0, 0, last * side, 2)
        strain_pass(w0, 0, (layers + 1) * side - 1, 1)
        near, far = edge_copies(side)
        first_update(last * side)
        near.start()
        first_update(1 + (last - 2) * side)
        far.start()

    loop(0, 2, first_edge)

    loop(1, 3, lambda i: strain_pass(w1, 1, i, 2, i + 1))
    loop(5, 7, lambda i: strain_pass(w1, 1, i, 2, i - 1))
    send_terms(1, 2, 4)
    loop(2, 6, second_update)

    def forward_edge(n):
        side = face(n)
        arrival(side, 4).wait_recv()
        strain_pass(w0, 0, last * side, 0, 6 + side)

    loop(0, 2, forward_edge)

    def terms_copy(side, k):
        dest = lax.rem(me_e + k, ne)
        m = (2 + side) * ne + k
        return remote(
            part.at[dest, pl.ds(6 + side, 1)], got.at[k, pl.ds(6 + side, 1)],
            rsend.at[m], rrecv.at[m], {"event": dest},
        )

    def second_edge(n):
        side = face(n)
        edge_copy(2, 1 + (layers + 1) * side, side, left).wait_recv()
        arrival(side, 5).wait_recv()
        strain_pass(w1, 1, last * side, 2, 6 + side)
        for k in range(1, ne):
            terms_copy(side, k).start()

    loop(0, 2, second_edge)
    for side in (0, 1):
        for k in range(1, ne):
            sums.append(terms_copy(side, k))
    for side in (0, 1):
        edge_copy(2, (layers + 3) * side, 2 + side, left).wait_recv()
    loop(0, 2, lambda t: strain_pass(w1, 1, (layers + 1) * t - 1, 1))
    loop(0, 2, second_update)
    loop(6, 8, second_update)

    mine = pl.ds(pl.multiple_of(me_e * band, band), band)
    inside = 2 * (ne - 1)
    for p, i in enumerate((3, 4, 1, 2, 5, 6, 0, 7)):
        if p == 0:
            for c in sums[:inside]:
                c.wait_recv()
        if p == 6:
            for c in sums[inside:]:
                c.wait_recv()
        con = part[me_e, p, 0]
        bulk = part[me_e, p, 1]
        for k in range(1, ne):
            con = con + got[k, p, 0]
            bulk = bulk + got[k, p, 1]
        m = md[1, i + 1, mine, :]
        sh[i] = (-0.5 * time_step) * m * con
        bk[i] = (-0.25 * time_step) * (md[0, i + 1, mine, :] + (2.0 / 3.0) * m) * bulk

    for side in (0, 1):
        for c in halo[side][:3]:
            c.wait_send()

    @pl.when(at_edge)
    def _():
        for c in handed + onward:
            c.wait_send()

    @pl.when(jnp.logical_not(is_tail))
    def _():
        for c in halo[0][3:]:
            c.wait_send()

    @pl.when(jnp.logical_not(is_head))
    def _():
        for c in halo[1][3:]:
            c.wait_send()

    for side in (0, 1):
        for c in edge_copies(side):
            c.wait_send()
    for c in sums:
        c.wait_send()


def put_out(field, shear, bulk, field_out, shear_out, bulk_out, sem):
    copies = [
        pltpu.make_async_copy(field, field_out.at[0], sem.at[0]),
        pltpu.make_async_copy(shear, shear_out, sem.at[1]),
        pltpu.make_async_copy(bulk, bulk_out, sem.at[2]),
    ]
    for c in copies:
        c.start()
    for c in copies:
        c.wait()


def local(nb, ne, adjoint_now, adjoint_prev, forward_field, density, lame_first, shear_modulus):
    layers, height, width = density.shape
    tall = height + 2 * PAD
    band = height // ne
    run = 16 if nb % 16 == 0 else 2
    f32 = jnp.float32
    dma = pltpu.SemaphoreType.DMA
    anywhere = pl.BlockSpec(memory_space=pl.ANY)
    vmem = pl.BlockSpec(memory_space=pltpu.VMEM)
    results = pl.pallas_call(
        functools.partial(kernel, nb, ne, run),
        out_shape=(
            pltpu.VMEM((3, layers, height, width), f32),
            pltpu.VMEM((layers, band, width), f32),
            pltpu.VMEM((layers, band, width), f32),
        ),
        in_specs=[anywhere] * 6,
        out_specs=(vmem,) * 3,
        scratch_shapes=[
            pltpu.VMEM((3, layers + 4, tall, width), f32),
            pltpu.VMEM((3, layers + 4, tall, width), f32),
            pltpu.VMEM((3, layers, height, width), f32),
            pltpu.VMEM((2, 3, layers + 2, tall, width), f32),
            pltpu.VMEM((2, layers + 2, height, width), f32),
            pltpu.VMEM((layers, height, width), f32),
            pltpu.VMEM((layers + 2, height, width), f32),
            pltpu.VMEM((layers + 2, tall, width), f32),
            pltpu.VMEM((layers + 2, height, width), f32),
            pltpu.VMEM((layers, tall, width), f32),
            pltpu.VMEM((layers, tall, width), f32),
            pltpu.VMEM((layers, height, width), f32),
            pltpu.VMEM((ne, layers, 2, band, width), f32),
            pltpu.VMEM((ne, layers, 2, band, width), f32),
            pltpu.VMEM((2, 3, 1, height, width), f32),
            pltpu.VMEM((3, 1, height, width), f32),
            dma((7,)),
            dma((12,)),
            dma((12,)),
            dma((4,)),
            dma((4,)),
            dma((4 * ne,)),
            dma((4 * ne,)),
            dma((3,)),
            dma((3,)),
            dma((3,)),
        ],
        compiler_params=pltpu.CompilerParams(collective_id=0, has_side_effects=True),
        name="adjoint",
    )(adjoint_now, adjoint_prev, forward_field, density, lame_first, shear_modulus)
    return pl.pallas_call(
        put_out,
        out_shape=(
            jax.ShapeDtypeStruct((1, 3, layers, height, width), f32),
            jax.ShapeDtypeStruct((layers, band, width), f32),
            jax.ShapeDtypeStruct((layers, band, width), f32),
        ),
        in_specs=[anywhere] * 3,
        out_specs=(anywhere,) * 3,
        scratch_shapes=[dma((3,))],
        compiler_params=pltpu.CompilerParams(vmem_limit_bytes=1 << 20),
        name="put_out",
    )(*results)


def solution(mesh):
    in_specs = (
        P("event", None, "blk", None, None),
        P("event", None, "blk", None, None),
        P("event", None, None, "blk", None, None),
        P("blk", None, None),
        P("blk", None, None),
        P("blk", None, None),
    )
    out_specs = (
        P("event", None, "blk", None, None),
        P("blk", "event", None),
        P("blk", "event", None),
    )
    body = functools.partial(local, mesh.shape["blk"], mesh.shape["event"])
    return jax.shard_map(body, mesh=mesh, in_specs=in_specs, out_specs=out_specs, check_vma=False)
```
